128 devices in a mesh: row: 8 (over z, core), col: 16 (over y, x).
Axes of the slice: x: 4, y: 4, z: 4, core: 2. Of those that a mesh axis runs over, the one named last changes fastest.
Arguments:
- kernel: float32 [16384, 16384], P('row', 'col'), may hold values from 0 to 3, as said below
Outputs:
- trailing: float32 [16384, 16384], P('row', 'col')
- factor_t: float32 [1024, 16384], P('col', 'row')
The draws below stay inside these ranges and needn't reach their ends.
Inputs may be any that keep to these rules, and one draw needn't show every extreme that they name: K is symmetric: an RBF kernel over 256 donor features plus each donor's noise variance, of 0.5 or more, on the diagonal.
All inputs are finite; a program needn't handle non-finite values.
Results may differ from the reference program's by a relative error of at most 0.0003.
Values sent between devices are 32-bit elements; how exact they have to be, the bound alone decides.
A program may use at most 128 MiB of HBM per device.

```python
import jax
import jax.numpy as jnp
from jax import lax

ORDER = 16384
FEAT = 256
PANEL = 512
PANELS = 2
TILE = 32
N_ROW = 8
N_COL = 16


def draw_kernel(key, part):
    feat_key = jax.random.fold_in(key, 11)
    scale_key = jax.random.fold_in(key, 23)
    noise_key = jax.random.fold_in(key, 37)
    feats = jax.random.normal(feat_key, (ORDER, FEAT), jnp.float32)
    scales = jnp.exp(jax.random.uniform(scale_key, (FEAT,), jnp.float32, jnp.log(0.001), jnp.log(0.006)))
    noise = jnp.exp(jax.random.uniform(noise_key, (ORDER,), jnp.float32, jnp.log(0.5), jnp.log(2.0)))
    weighted = feats * scales
    norms = jnp.sum(feats * weighted, axis=1)
    cross = jnp.dot(weighted, feats.T, precision=lax.Precision.HIGHEST, preferred_element_type=jnp.float32)
    dense = jnp.exp(-jnp.maximum(norms[:, None] + norms[None, :] - 2.0 * cross, 0.0))
    positions = jnp.arange(ORDER, dtype=jnp.int32)
    dense = dense + jnp.where(positions[:, None] == positions[None, :], noise[:, None], 0.0)
    stored = dense.reshape(ORDER // (N_ROW * TILE), N_ROW, TILE, ORDER // (N_COL * TILE), N_COL, TILE)
    return stored.transpose(1, 0, 2, 4, 3, 5).reshape(ORDER, ORDER)


def setup_inputs(seed: int = 0) -> dict:
    key_list = jax.random.split(jax.random.key(seed), 2)
    kernel = draw_kernel(jax.random.fold_in(key_list[1], 71), 0)
    return dict(kernel=kernel)


def reference(kernel):
    highest = lax.Precision.HIGHEST
    schur = kernel.reshape(N_ROW, ORDER // (N_ROW * TILE), TILE, N_COL, ORDER // (N_COL * TILE), TILE)
    schur = schur.transpose(1, 0, 2, 4, 3, 5).reshape(ORDER, ORDER)
    positions = jnp.arange(ORDER, dtype=jnp.int32)
    factors = []
    for panel_idx in range(PANELS):
        first_col = panel_idx * PANEL
        corner = schur[first_col:first_col + PANEL, first_col:first_col + PANEL]
        lower_fac = jnp.linalg.cholesky(corner)
        solved = jax.scipy.linalg.solve_triangular(lower_fac, schur[:, first_col:first_col + PANEL].T, lower=True)
        solved = jnp.where(positions[None, :] >= first_col, solved, 0.0)
        schur = schur - jnp.dot(solved.T.astype(jnp.float32), solved.astype(jnp.float32), precision=highest, preferred_element_type=jnp.float32)
        factors.append(solved)
    limit = PANELS * PANEL
    keep = (positions[:, None] >= limit) & (positions[None, :] >= limit)
    schur = jnp.where(keep, schur, 0.0)
    trailing = schur.reshape(ORDER // (N_ROW * TILE), N_ROW, TILE, ORDER // (N_COL * TILE), N_COL, TILE)
    trailing = trailing.transpose(1, 0, 2, 4, 3, 5).reshape(ORDER, ORDER)
    stacked = jnp.concatenate(factors, axis=0)
    stacked = stacked.reshape(PANELS * PANEL, ORDER // (N_ROW * TILE), N_ROW, TILE)
    stacked = stacked.transpose(0, 2, 1, 3).reshape(PANELS * PANEL, ORDER)
    return (trailing, stacked)
```

```python
import jax
import jax.numpy as jnp
from jax import lax
from jax.sharding import PartitionSpec as P

PANEL = 512
PANELS = 2
TILE = 32

HIGHEST = lax.Precision.HIGHEST


def mm(a, b):
    return jnp.dot(a, b, precision=HIGHEST, preferred_element_type=jnp.float32)


def mm_tn(a, b):
    return lax.dot_general(
        a, b, (((0,), (0,)), ((), ())), precision=HIGHEST, preferred_element_type=jnp.float32
    )


def mm_nt(a, b):
    return lax.dot_general(
        a, b, (((1,), (1,)), ((), ())), precision=HIGHEST, preferred_element_type=jnp.float32
    )


def tri_inverse(lower):
    eye = jnp.eye(lower.shape[0], dtype=lower.dtype)
    return jax.scipy.linalg.solve_triangular(lower, eye, lower=True)


def sym_chol(block):
    return jnp.linalg.cholesky(block)


def local(kernel):
    grid_rows = lax.axis_size("row")
    grid_cols = lax.axis_size("col")
    my_row = lax.axis_index("row")
    my_col = lax.axis_index("col")
    rows_loc, cols_loc = kernel.shape
    lead = PANELS * PANEL
    lead_rt = lead // (TILE * grid_rows)
    lead_ct = lead // (TILE * grid_cols)
    lead_r = lead_rt * TILE
    lead_c = lead_ct * TILE

    row_local = jnp.arange(rows_loc, dtype=jnp.int32)
    row_ids = (row_local // TILE * grid_rows + my_row) * TILE + row_local % TILE
    col_local = jnp.arange(cols_loc, dtype=jnp.int32)
    col_ids = (col_local // TILE * grid_cols + my_col) * TILE + col_local % TILE

    corner = kernel[:lead_r, :lead_c].reshape(1, lead_r * lead_c)
    blocks = lax.all_gather(corner, ("row", "col"), axis=0, tiled=True)
    blocks = blocks.reshape(grid_rows, grid_cols, lead_rt, TILE, lead_ct, TILE)
    a_lead = blocks.transpose(2, 0, 3, 4, 1, 5).reshape(lead, lead)

    cols_part = lax.all_gather(kernel[:, :lead_c], "col", axis=1, tiled=True)
    cols_part = cols_part.reshape(rows_loc, grid_cols, lead_ct, TILE)
    x_rows = cols_part.transpose(0, 2, 1, 3).reshape(rows_loc, lead)

    rows_part = lax.all_gather(kernel[:lead_r, :], "row", axis=0, tiled=True)
    rows_part = rows_part.reshape(grid_rows, lead_rt, TILE, cols_loc)
    y_cols = rows_part.transpose(1, 0, 2, 3).reshape(lead, cols_loc)

    a00 = a_lead[:PANEL, :PANEL]
    a01 = a_lead[:PANEL, PANEL:]
    a11 = a_lead[PANEL:, PANEL:]
    l0 = sym_chol(a00)
    l0inv = tri_inverse(l0)
    g0p1 = mm(l0inv, a01)
    s11 = a11 - mm_tn(g0p1, g0p1)
    l1 = sym_chol(s11)
    l1inv = tri_inverse(l1)

    def factor(panel_t, ids):
        g0 = mm(l0inv, panel_t[:PANEL])
        s1 = panel_t[PANEL:] - mm_tn(g0p1, g0)
        g1 = mm(l1inv, s1)
        g1 = jnp.where(ids[None, :] >= PANEL, g1, 0.0)
        return jnp.concatenate([g0, g1], axis=0)

    g_rows = factor(x_rows.T, row_ids)
    g_cols = factor(y_cols, col_ids)

    schur = kernel - mm_tn(g_rows, g_cols)
    keep = (row_ids[:, None] >= lead) & (col_ids[None, :] >= lead)
    trailing = jnp.where(keep, schur, 0.0)
    per_col = lead // grid_cols
    factor_out = lax.dynamic_slice_in_dim(g_rows, my_col * per_col, per_col, 0)
    return (trailing, factor_out)


def solution(mesh):
    return jax.shard_map(
        local,
        mesh=mesh,
        in_specs=(P("row", "col"),),
        out_specs=(P("row", "col"), P("col", "row")),
        check_vma=False,
    )
```

```python
import jax
import jax.numpy as jnp
from jax import lax
from jax.experimental import pallas as pl
from jax.experimental.pallas import tpu as pltpu
from jax.sharding import PartitionSpec as P

PANEL = 512
PANELS = 2
TILE = 32
BLK = 128

HIGHEST = lax.Precision.HIGHEST


def _mm(a, b):
    return jnp.dot(a, b, precision=HIGHEST, preferred_element_type=jnp.float32)


def _diag_factor(d, lt_ref, w_ref):
    sub = lax.broadcasted_iota(jnp.int32, (BLK, BLK), 0)
    lane = lax.broadcasted_iota(jnp.int32, (BLK, BLK), 1)
    lane_row = lax.broadcasted_iota(jnp.int32, (1, BLK), 1)
    w0 = (sub == lane).astype(jnp.float32)

    def step(j, carry):
        dm, wm = carry
        rowsel = sub == j
        rowj = jnp.sum(jnp.where(rowsel, dm, 0.0), axis=0, keepdims=True)
        colj = jnp.sum(jnp.where(lane == j, dm, 0.0), axis=1, keepdims=True)
        piv = jnp.sum(jnp.where(lane_row == j, rowj, 0.0), axis=1, keepdims=True)
        inv = lax.rsqrt(piv)
        lrow = jnp.where(lane_row >= j, rowj * inv, 0.0)
        lcol = jnp.where(sub[:, 0:1] > j, colj * inv, 0.0)
        dm = dm - lcol * lrow
        wj = jnp.sum(jnp.where(rowsel, wm, 0.0), axis=0, keepdims=True) * inv
        wm = jnp.where(rowsel, wj, wm - lcol * wj)
        lt_ref[pl.ds(j, 1), :] = lrow
        return dm, wm

    _, wm = lax.fori_loop(0, BLK, step, (d, w0))
    w_ref[...] = wm


def _chol_inv_kernel(a_ref, linv_ref, work, lt, dblk):
    n = a_ref.shape[0]
    nb = n // BLK
    work[...] = a_ref[...]
    linv_ref[...] = jnp.zeros_like(linv_ref)
    for k in range(nb):
        s = k * BLK
        _diag_factor(work[s:s + BLK, s:s + BLK], dblk, linv_ref.at[s:s + BLK, s:s + BLK])
        lt[s:s + BLK, s:s + BLK] = dblk[...]
        if k < nb - 1:
            e = s + BLK
            u = _mm(linv_ref[s:s + BLK, s:s + BLK], work[s:s + BLK, e:])
            lt[s:s + BLK, e:] = u
            work[e:, e:] = work[e:, e:] - _mm(u.T, u)
    for i in range(1, nb):
        s = i * BLK
        li = lt[0:s, s:s + BLK].T
        acc = _mm(li, linv_ref[0:s, 0:s])
        linv_ref[s:s + BLK, 0:s] = -_mm(linv_ref[s:s + BLK, s:s + BLK], acc)


def chol_inv(a):
    n = a.shape[0]
    return pl.pallas_call(
        _chol_inv_kernel,
        out_shape=jax.ShapeDtypeStruct((n, n), jnp.float32),
        in_specs=[pl.BlockSpec(memory_space=pltpu.VMEM)],
        out_specs=pl.BlockSpec(memory_space=pltpu.VMEM),
        scratch_shapes=[
            pltpu.VMEM((n, n), jnp.float32),
            pltpu.VMEM((n, n), jnp.float32),
            pltpu.VMEM((BLK, BLK), jnp.float32),
        ],
        compiler_params=pltpu.CompilerParams(vmem_limit_bytes=60 * 1024 * 1024),
    )(a)


def mm(a, b):
    return jnp.dot(a, b, precision=HIGHEST, preferred_element_type=jnp.float32)


def mm_tn(a, b):
    return lax.dot_general(
        a, b, (((0,), (0,)), ((), ())), precision=HIGHEST, preferred_element_type=jnp.float32
    )


def tiles_to_matrix(x, outer, inner):
    rest = x.shape[1:]
    x = x.reshape((outer, inner, TILE) + rest)
    return jnp.swapaxes(x, 0, 1).reshape((outer * inner * TILE,) + rest)


def local(kernel):
    grid_rows = lax.axis_size("row")
    grid_cols = lax.axis_size("col")
    my_row = lax.axis_index("row")
    my_col = lax.axis_index("col")
    rows_loc, cols_loc = kernel.shape
    lead = PANELS * PANEL
    lead_rt = lead // (TILE * grid_rows)
    lead_ct = lead // (TILE * grid_cols)
    lead_r = lead_rt * TILE
    lead_c = lead_ct * TILE

    row_local = jnp.arange(rows_loc, dtype=jnp.int32)
    row_ids = (row_local // TILE * grid_rows + my_row) * TILE + row_local % TILE
    col_local = jnp.arange(cols_loc, dtype=jnp.int32)
    col_ids = (col_local // TILE * grid_cols + my_col) * TILE + col_local % TILE

    corner = lax.all_gather(kernel[:lead_r, :lead_c], "col", axis=1, tiled=True)
    corner = lax.all_gather(corner, "row", axis=0, tiled=True)
    corner = tiles_to_matrix(corner, grid_rows, lead_rt)
    a_lead = tiles_to_matrix(corner.T, grid_cols, lead_ct)

    cols_part = lax.all_gather(kernel[:, :lead_c], "col", axis=1, tiled=True)
    x_rows_t = tiles_to_matrix(cols_part.T, grid_cols, lead_ct)

    rows_part = lax.all_gather(kernel[:lead_r, :], "row", axis=0, tiled=True)
    y_cols = tiles_to_matrix(rows_part, grid_rows, lead_rt)

    linv = chol_inv(a_lead)
    l0inv = linv[:PANEL, :PANEL]
    l1row = linv[PANEL:, :]

    def factor(panel_t, ids):
        g0 = mm(l0inv, panel_t[:PANEL])
        g1 = mm(l1row, panel_t)
        g1 = jnp.where(ids[None, :] >= PANEL, g1, 0.0)
        return jnp.concatenate([g0, g1], axis=0)

    g_rows = factor(x_rows_t, row_ids)
    g_cols = factor(y_cols, col_ids)

    schur = kernel - mm_tn(g_rows, g_cols)
    keep = (row_ids[:, None] >= lead) & (col_ids[None, :] >= lead)
    trailing = jnp.where(keep, schur, 0.0)
    per_col = lead // grid_cols
    factor_out = lax.dynamic_slice_in_dim(g_rows, my_col * per_col, per_col, 0)
    return (trailing, factor_out)


def solution(mesh):
    return jax.shard_map(
        local,
        mesh=mesh,
        in_specs=(P("row", "col"),),
        out_specs=(P("row", "col"), P("col", "row")),
        check_vma=False,
    )
```

```python
import jax
import jax.numpy as jnp
from jax import lax
from jax.experimental import pallas as pl
from jax.experimental.pallas import tpu as pltpu
from jax.sharding import PartitionSpec as P

PANEL = 512
PANELS = 2
TILE = 32
BLK = 128

HIGHEST = lax.Precision.HIGHEST


def _mm(a, b):
    return jnp.dot(a, b, precision=HIGHEST, preferred_element_type=jnp.float32)


def _diag_factor(d, lt_ref, w_ref):
    sub = lax.broadcasted_iota(jnp.int32, (BLK, BLK), 0)
    lane = lax.broadcasted_iota(jnp.int32, (BLK, BLK), 1)
    lane_row = lax.broadcasted_iota(jnp.int32, (1, BLK), 1)
    w0 = (sub == lane).astype(jnp.float32)

    def step(j, carry):
        dm, wm = carry
        rowsel = sub == j
        rowj = jnp.sum(jnp.where(rowsel, dm, 0.0), axis=0, keepdims=True)
        colj = jnp.sum(jnp.where(lane == j, dm, 0.0), axis=1, keepdims=True)
        piv = jnp.sum(jnp.where(lane_row == j, rowj, 0.0), axis=1, keepdims=True)
        inv = lax.rsqrt(piv)
        lrow = jnp.where(lane_row >= j, rowj * inv, 0.0)
        lcol = jnp.where(sub[:, 0:1] > j, colj * inv, 0.0)
        dm = dm - lcol * lrow
        wj = jnp.sum(jnp.where(rowsel, wm, 0.0), axis=0, keepdims=True) * inv
        wm = jnp.where(rowsel, wj, wm - lcol * wj)
        lt_ref[pl.ds(j, 1), :] = lrow
        return dm, wm

    _, wm = lax.fori_loop(0, BLK, step, (d, w0))
    w_ref[...] = wm


def _chol_inv_kernel(a_ref, linv_ref, work, lt, dblk):
    n = a_ref.shape[0]
    nb = n // BLK
    work[...] = a_ref[...]
    linv_ref[...] = jnp.zeros_like(linv_ref)
    for k in range(nb):
        s = k * BLK
        _diag_factor(work[s:s + BLK, s:s + BLK], dblk, linv_ref.at[s:s + BLK, s:s + BLK])
        lt[s:s + BLK, s:s + BLK] = dblk[...]
        if k < nb - 1:
            e = s + BLK
            u = _mm(linv_ref[s:s + BLK, s:s + BLK], work[s:s + BLK, e:])
            lt[s:s + BLK, e:] = u
            work[e:, e:] = work[e:, e:] - _mm(u.T, u)
    for i in range(1, nb):
        s = i * BLK
        li = lt[0:s, s:s + BLK].T
        acc = _mm(li, linv_ref[0:s, 0:s])
        linv_ref[s:s + BLK, 0:s] = -_mm(linv_ref[s:s + BLK, s:s + BLK], acc)


def chol_inv(a):
    n = a.shape[0]
    return pl.pallas_call(
        _chol_inv_kernel,
        out_shape=jax.ShapeDtypeStruct((n, n), jnp.float32),
        in_specs=[pl.BlockSpec(memory_space=pltpu.VMEM)],
        out_specs=pl.BlockSpec(memory_space=pltpu.VMEM),
        scratch_shapes=[
            pltpu.VMEM((n, n), jnp.float32),
            pltpu.VMEM((n, n), jnp.float32),
            pltpu.VMEM((BLK, BLK), jnp.float32),
        ],
        compiler_params=pltpu.CompilerParams(vmem_limit_bytes=60 * 1024 * 1024),
    )(a)


def mm(a, b):
    return jnp.dot(a, b, precision=HIGHEST, preferred_element_type=jnp.float32)


def mm_tn(a, b, precision=HIGHEST):
    return lax.dot_general(
        a, b, (((0,), (0,)), ((), ())), precision=precision, preferred_element_type=jnp.float32
    )


def tiles_to_matrix(x, outer, inner):
    rest = x.shape[1:]
    x = x.reshape((outer, inner, TILE) + rest)
    return jnp.swapaxes(x, 0, 1).reshape((outer * inner * TILE,) + rest)


def local(kernel):
    grid_rows = lax.axis_size("row")
    grid_cols = lax.axis_size("col")
    my_row = lax.axis_index("row")
    my_col = lax.axis_index("col")
    rows_loc, cols_loc = kernel.shape
    lead = PANELS * PANEL
    lead_rt = lead // (TILE * grid_rows)
    lead_ct = lead // (TILE * grid_cols)
    lead_r = lead_rt * TILE
    lead_c = lead_ct * TILE

    row_local = jnp.arange(rows_loc, dtype=jnp.int32)
    row_ids = (row_local // TILE * grid_rows + my_row) * TILE + row_local % TILE
    col_local = jnp.arange(cols_loc, dtype=jnp.int32)
    col_ids = (col_local // TILE * grid_cols + my_col) * TILE + col_local % TILE

    corner = lax.all_gather(kernel[:lead_r, :lead_c], "col", axis=1, tiled=True)
    corner = lax.all_gather(corner, "row", axis=0, tiled=True)
    corner = tiles_to_matrix(corner, grid_rows, lead_rt)
    a_lead = tiles_to_matrix(corner.T, grid_cols, lead_ct)

    cols_part = lax.all_gather(kernel[:, :lead_c], "col", axis=1, tiled=True)
    x_rows_t = tiles_to_matrix(cols_part.T, grid_cols, lead_ct)

    rows_part = lax.all_gather(kernel[:lead_r, :], "row", axis=0, tiled=True)
    y_cols = tiles_to_matrix(rows_part, grid_rows, lead_rt)

    linv = chol_inv(a_lead)
    l0inv = linv[:PANEL, :PANEL]
    l1row = linv[PANEL:, :]

    def factor(panel_t, ids):
        g0 = mm(l0inv, panel_t[:PANEL])
        g1 = mm(l1row, panel_t)
        g1 = jnp.where(ids[None, :] >= PANEL, g1, 0.0)
        return jnp.concatenate([g0, g1], axis=0)

    g_rows = factor(x_rows_t, row_ids)
    g_cols = factor(y_cols, col_ids)

    schur = kernel - mm_tn(g_rows, g_cols, lax.Precision.HIGH)
    keep = (row_ids[:, None] >= lead) & (col_ids[None, :] >= lead)
    trailing = jnp.where(keep, schur, 0.0)
    per_col = lead // grid_cols
    factor_out = lax.dynamic_slice_in_dim(g_rows, my_col * per_col, per_col, 0)
    return (trailing, factor_out)


def solution(mesh):
    return jax.shard_map(
        local,
        mesh=mesh,
        in_specs=(P("row", "col"),),
        out_specs=(P("row", "col"), P("col", "row")),
        check_vma=False,
    )
```

```python
import jax
import jax.numpy as jnp
from jax import lax
from jax.experimental import pallas as pl
from jax.experimental.pallas import tpu as pltpu
from jax.sharding import PartitionSpec as P

PANEL = 512
PANELS = 2
TILE = 32
BLK = 128

HIGHEST = lax.Precision.HIGHEST


def _mm(a, b):
    return jnp.dot(a, b, precision=HIGHEST, preferred_element_type=jnp.float32)


def _diag_factor(d, lt_ref, w_ref):
    sub_all = lax.broadcasted_iota(jnp.int32, (BLK, BLK), 0)
    lane_all = lax.broadcasted_iota(jnp.int32, (BLK, BLK), 1)
    lane_row = lax.broadcasted_iota(jnp.int32, (1, BLK), 1)
    dm = d
    wm = (sub_all == lane_all).astype(jnp.float32)
    part = 8
    for q in range(BLK // part):
        lo = q * part
        rows = BLK - lo
        sub = lax.broadcasted_iota(jnp.int32, (rows, BLK), 0) + lo
        lane = lax.broadcasted_iota(jnp.int32, (rows, BLK), 1)

        def step(j, carry, sub=sub, lane=lane):
            dq, wq = carry
            rowsel = sub == j
            rowj = jnp.sum(jnp.where(rowsel, dq, 0.0), axis=0, keepdims=True)
            colj = jnp.sum(jnp.where(lane == j, dq, 0.0), axis=1, keepdims=True)
            piv = jnp.sum(jnp.where(lane_row == j, rowj, 0.0), axis=1, keepdims=True)
            inv = lax.rsqrt(piv)
            lrow = jnp.where(lane_row >= j, rowj * inv, 0.0)
            lcol = jnp.where(sub[:, 0:1] > j, colj * inv, 0.0)
            dq = dq - lcol * lrow
            wj = jnp.sum(jnp.where(rowsel, wq, 0.0), axis=0, keepdims=True) * inv
            wq = jnp.where(rowsel, wj, wq - lcol * wj)
            lt_ref[pl.ds(j, 1), :] = lrow
            return dq, wq

        dq, wq = lax.fori_loop(lo, lo + part, step, (dm[lo:], wm[lo:]))
        w_ref[lo:lo + part, :] = wq[:part]
        if q + 1 < BLK // part:
            dm = jnp.concatenate([jnp.zeros((lo + part, BLK), jnp.float32), dq[part:]], axis=0)
            wm = jnp.concatenate([jnp.zeros((lo + part, BLK), jnp.float32), wq[part:]], axis=0)


def _chol_inv_kernel(a_ref, linv_ref, work, lt, dblk):
    n = a_ref.shape[0]
    nb = n // BLK
    work[...] = a_ref[...]
    linv_ref[...] = jnp.zeros_like(linv_ref)
    for k in range(nb):
        s = k * BLK
        _diag_factor(work[s:s + BLK, s:s + BLK], dblk, linv_ref.at[s:s + BLK, s:s + BLK])
        lt[s:s + BLK, s:s + BLK] = dblk[...]
        if k < nb - 1:
            e = s + BLK
            u = _mm(linv_ref[s:s + BLK, s:s + BLK], work[s:s + BLK, e:])
            lt[s:s + BLK, e:] = u
            work[e:, e:] = work[e:, e:] - _mm(u.T, u)
    for i in range(1, nb):
        s = i * BLK
        li = lt[0:s, s:s + BLK].T
        acc = _mm(li, linv_ref[0:s, 0:s])
        linv_ref[s:s + BLK, 0:s] = -_mm(linv_ref[s:s + BLK, s:s + BLK], acc)


def chol_inv(a):
    n = a.shape[0]
    return pl.pallas_call(
        _chol_inv_kernel,
        out_shape=jax.ShapeDtypeStruct((n, n), jnp.float32),
        in_specs=[pl.BlockSpec(memory_space=pltpu.VMEM)],
        out_specs=pl.BlockSpec(memory_space=pltpu.VMEM),
        scratch_shapes=[
            pltpu.VMEM((n, n), jnp.float32),
            pltpu.VMEM((n, n), jnp.float32),
            pltpu.VMEM((BLK, BLK), jnp.float32),
        ],
        compiler_params=pltpu.CompilerParams(vmem_limit_bytes=60 * 1024 * 1024),
    )(a)


def mm(a, b):
    return jnp.dot(a, b, precision=HIGHEST, preferred_element_type=jnp.float32)


def mm_tn(a, b, precision=HIGHEST):
    return lax.dot_general(
        a, b, (((0,), (0,)), ((), ())), precision=precision, preferred_element_type=jnp.float32
    )


def tiles_to_matrix(x, outer, inner):
    rest = x.shape[1:]
    x = x.reshape((outer, inner, TILE) + rest)
    return jnp.swapaxes(x, 0, 1).reshape((outer * inner * TILE,) + rest)


def local(kernel):
    grid_rows = lax.axis_size("row")
    grid_cols = lax.axis_size("col")
    my_row = lax.axis_index("row")
    my_col = lax.axis_index("col")
    rows_loc, cols_loc = kernel.shape
    lead = PANELS * PANEL
    lead_rt = lead // (TILE * grid_rows)
    lead_ct = lead // (TILE * grid_cols)
    lead_r = lead_rt * TILE
    lead_c = lead_ct * TILE

    row_local = jnp.arange(rows_loc, dtype=jnp.int32)
    row_ids = (row_local // TILE * grid_rows + my_row) * TILE + row_local % TILE
    col_local = jnp.arange(cols_loc, dtype=jnp.int32)
    col_ids = (col_local // TILE * grid_cols + my_col) * TILE + col_local % TILE

    corner = lax.all_gather(kernel[:lead_r, :lead_c], "col", axis=1, tiled=True)
    corner = lax.all_gather(corner, "row", axis=0, tiled=True)
    corner = tiles_to_matrix(corner, grid_rows, lead_rt)
    a_lead = tiles_to_matrix(corner.T, grid_cols, lead_ct)

    cols_part = lax.all_gather(kernel[:, :lead_c], "col", axis=1, tiled=True)
    x_rows_t = tiles_to_matrix(cols_part.T, grid_cols, lead_ct)

    rows_part = lax.all_gather(kernel[:lead_r, :], "row", axis=0, tiled=True)
    y_cols = tiles_to_matrix(rows_part, grid_rows, lead_rt)

    linv = chol_inv(a_lead)
    l0inv = linv[:PANEL, :PANEL]
    l1row = linv[PANEL:, :]

    def factor(panel_t, ids):
        g0 = mm(l0inv, panel_t[:PANEL])
        g1 = mm(l1row, panel_t)
        g1 = jnp.where(ids[None, :] >= PANEL, g1, 0.0)
        return jnp.concatenate([g0, g1], axis=0)

    g_rows = factor(x_rows_t, row_ids)
    g_cols = factor(y_cols, col_ids)

    schur = kernel - mm_tn(g_rows, g_cols, lax.Precision.HIGH)
    keep = (row_ids[:, None] >= lead) & (col_ids[None, :] >= lead)
    trailing = jnp.where(keep, schur, 0.0)
    per_col = lead // grid_cols
    factor_out = lax.dynamic_slice_in_dim(g_rows, my_col * per_col, per_col, 0)
    return (trailing, factor_out)


def solution(mesh):
    return jax.shard_map(
        local,
        mesh=mesh,
        in_specs=(P("row", "col"),),
        out_specs=(P("row", "col"), P("col", "row")),
        check_vma=False,
    )
```

```python
import jax
import jax.numpy as jnp
from jax import lax
from jax.experimental import pallas as pl
from jax.experimental.pallas import tpu as pltpu
from jax.sharding import PartitionSpec as P

PANEL = 512
PANELS = 2
TILE = 32
BLK = 128

HIGHEST = lax.Precision.HIGHEST


def _mm(a, b):
    return jnp.dot(a, b, precision=HIGHEST, preferred_element_type=jnp.float32)


def _diag_factor(d, lt_ref, w_ref):
    sub_all = lax.broadcasted_iota(jnp.int32, (BLK, BLK), 0)
    lane_all = lax.broadcasted_iota(jnp.int32, (BLK, BLK), 1)
    lane_row = lax.broadcasted_iota(jnp.int32, (1, BLK), 1)
    dm = d
    wm = (sub_all == lane_all).astype(jnp.float32)
    part = 8
    for q in range(BLK // part):
        lo = q * part
        rows = BLK - lo
        sub = lax.broadcasted_iota(jnp.int32, (rows, BLK), 0) + lo
        lane = lax.broadcasted_iota(jnp.int32, (rows, BLK), 1)

        def step(j, carry, sub=sub, lane=lane):
            dq, wq = carry
            rowsel = sub == j
            rowj = jnp.sum(jnp.where(rowsel, dq, 0.0), axis=0, keepdims=True)
            colj = jnp.sum(jnp.where(lane == j, dq, 0.0), axis=1, keepdims=True)
            piv = jnp.sum(jnp.where(lane_row == j, rowj, 0.0), axis=1, keepdims=True)
            inv = lax.rsqrt(piv)
            lrow = jnp.where(lane_row >= j, rowj * inv, 0.0)
            lcol = jnp.where(sub[:, 0:1] > j, colj * inv, 0.0)
            dq = dq - lcol * lrow
            wj = jnp.sum(jnp.where(rowsel, wq, 0.0), axis=0, keepdims=True) * inv
            wq = jnp.where(rowsel, wj, wq - lcol * wj)
            lt_ref[pl.ds(j, 1), :] = lrow
            return dq, wq

        dq, wq = lax.fori_loop(lo, lo + part, step, (dm[lo:], wm[lo:]))
        w_ref[lo:lo + part, :] = wq[:part]
        if q + 1 < BLK // part:
            dm = jnp.concatenate([jnp.zeros((lo + part, BLK), jnp.float32), dq[part:]], axis=0)
            wm = jnp.concatenate([jnp.zeros((lo + part, BLK), jnp.float32), wq[part:]], axis=0)


def _chol_inv_kernel(a_ref, linv_ref, work, lt, dblk):
    n = a_ref.shape[0]
    nb = n // BLK
    work[...] = a_ref[...]
    linv_ref[...] = jnp.zeros_like(linv_ref)
    for k in range(nb):
        s = k * BLK
        _diag_factor(work[s:s + BLK, s:s + BLK], dblk, linv_ref.at[s:s + BLK, s:s + BLK])
        lt[s:s + BLK, s:s + BLK] = dblk[...]
        if k < nb - 1:
            e = s + BLK
            u = _mm(linv_ref[s:s + BLK, s:s + BLK], work[s:s + BLK, e:])
            lt[s:s + BLK, e:] = u
            work[e:, e:] = work[e:, e:] - _mm(u.T, u)
    for i in range(1, nb):
        s = i * BLK
        li = lt[0:s, s:s + BLK].T
        acc = _mm(li, linv_ref[0:s, 0:s])
        linv_ref[s:s + BLK, 0:s] = -_mm(linv_ref[s:s + BLK, s:s + BLK], acc)


def chol_inv(a):
    n = a.shape[0]
    return pl.pallas_call(
        _chol_inv_kernel,
        out_shape=jax.ShapeDtypeStruct((n, n), jnp.float32),
        in_specs=[pl.BlockSpec(memory_space=pltpu.VMEM)],
        out_specs=pl.BlockSpec(memory_space=pltpu.VMEM),
        scratch_shapes=[
            pltpu.VMEM((n, n), jnp.float32),
            pltpu.VMEM((n, n), jnp.float32),
            pltpu.VMEM((BLK, BLK), jnp.float32),
        ],
        compiler_params=pltpu.CompilerParams(vmem_limit_bytes=60 * 1024 * 1024),
    )(a)


def mm(a, b):
    return jnp.dot(a, b, precision=HIGHEST, preferred_element_type=jnp.float32)


def mm_tn(a, b, precision=HIGHEST):
    return lax.dot_general(
        a, b, (((0,), (0,)), ((), ())), precision=precision, preferred_element_type=jnp.float32
    )


def tiles_to_matrix(x, outer, inner):
    rest = x.shape[1:]
    x = x.reshape((outer, inner, TILE) + rest)
    return jnp.swapaxes(x, 0, 1).reshape((outer * inner * TILE,) + rest)


def local(kernel):
    grid_rows = lax.axis_size("row")
    grid_cols = lax.axis_size("col")
    my_row = lax.axis_index("row")
    my_col = lax.axis_index("col")
    rows_loc, cols_loc = kernel.shape
    lead = PANELS * PANEL
    lead_rt = lead // (TILE * grid_rows)
    lead_ct = lead // (TILE * grid_cols)
    lead_r = lead_rt * TILE
    lead_c = lead_ct * TILE

    row_local = jnp.arange(rows_loc, dtype=jnp.int32)
    row_ids = (row_local // TILE * grid_rows + my_row) * TILE + row_local % TILE
    col_local = jnp.arange(cols_loc, dtype=jnp.int32)
    col_ids = (col_local // TILE * grid_cols + my_col) * TILE + col_local % TILE

    corner = kernel[:lead_r, :lead_c].reshape(1, lead_r * lead_c)
    corner = lax.all_gather(corner, ("row", "col"), axis=0, tiled=True)
    corner = corner.reshape(grid_rows, grid_cols, lead_r, lead_c).transpose(0, 2, 1, 3)
    corner = tiles_to_matrix(corner.reshape(lead, lead), grid_rows, lead_rt)
    a_lead = tiles_to_matrix(corner.T, grid_cols, lead_ct)

    cols_part = lax.all_gather(kernel[:, :lead_c], "col", axis=1, tiled=True)
    x_rows_t = tiles_to_matrix(cols_part.T, grid_cols, lead_ct)

    rows_part = lax.all_gather(kernel[:lead_r, :], "row", axis=0, tiled=True)
    y_cols = tiles_to_matrix(rows_part, grid_rows, lead_rt)

    linv = chol_inv(a_lead)
    l0inv = linv[:PANEL, :PANEL]
    l1row = linv[PANEL:, :]

    def factor(panel_t, ids):
        g0 = mm(l0inv, panel_t[:PANEL])
        g1 = mm(l1row, panel_t)
        g1 = jnp.where(ids[None, :] >= PANEL, g1, 0.0)
        return jnp.concatenate([g0, g1], axis=0)

    g_rows = factor(x_rows_t, row_ids)
    g_cols = factor(y_cols, col_ids)

    schur = kernel - mm_tn(g_rows, g_cols, lax.Precision.HIGH)
    keep = (row_ids[:, None] >= lead) & (col_ids[None, :] >= lead)
    trailing = jnp.where(keep, schur, 0.0)
    per_col = lead // grid_cols
    factor_out = lax.dynamic_slice_in_dim(g_rows, my_col * per_col, per_col, 0)
    return (trailing, factor_out)


def solution(mesh):
    return jax.shard_map(
        local,
        mesh=mesh,
        in_specs=(P("row", "col"),),
        out_specs=(P("row", "col"), P("col", "row")),
        check_vma=False,
    )
```

```python
import jax
import jax.numpy as jnp
from jax import lax
from jax.experimental import pallas as pl
from jax.experimental.pallas import tpu as pltpu
from jax.sharding import PartitionSpec as P

PANEL = 512
PANELS = 2
TILE = 32
BLK = 128

HIGHEST = lax.Precision.HIGHEST


def _mm(a, b):
    return jnp.dot(a, b, precision=HIGHEST, preferred_element_type=jnp.float32)


def _diag_factor(d, lt_ref, w_ref):
    sub_all = lax.broadcasted_iota(jnp.int32, (BLK, BLK), 0)
    lane_all = lax.broadcasted_iota(jnp.int32, (BLK, BLK), 1)
    lane_row = lax.broadcasted_iota(jnp.int32, (1, BLK), 1)
    dm = d
    wm = (sub_all == lane_all).astype(jnp.float32)
    part = 8
    for q in range(BLK // part):
        lo = q * part
        rows = BLK - lo
        sub = lax.broadcasted_iota(jnp.int32, (rows, BLK), 0) + lo
        lane = lax.broadcasted_iota(jnp.int32, (rows, BLK), 1)

        def step(j, carry, sub=sub, lane=lane):
            dq, wq = carry
            rowsel = sub == j
            rowj = jnp.sum(jnp.where(rowsel, dq, 0.0), axis=0, keepdims=True)
            colj = jnp.sum(jnp.where(lane == j, dq, 0.0), axis=1, keepdims=True)
            piv = jnp.sum(jnp.where(lane_row == j, rowj, 0.0), axis=1, keepdims=True)
            inv = lax.rsqrt(piv)
            lrow = jnp.where(lane_row >= j, rowj * inv, 0.0)
            lcol = jnp.where(sub[:, 0:1] > j, colj * inv, 0.0)
            dq = dq - lcol * lrow
            wj = jnp.sum(jnp.where(rowsel, wq, 0.0), axis=0, keepdims=True) * inv
            wq = jnp.where(rowsel, wj, wq - lcol * wj)
            lt_ref[pl.ds(j, 1), :] = lrow
            return dq, wq

        dq, wq = lax.fori_loop(lo, lo + part, step, (dm[lo:], wm[lo:]))
        w_ref[lo:lo + part, :] = wq[:part]
        if q + 1 < BLK // part:
            dm = jnp.concatenate([jnp.zeros((lo + part, BLK), jnp.float32), dq[part:]], axis=0)
            wm = jnp.concatenate([jnp.zeros((lo + part, BLK), jnp.float32), wq[part:]], axis=0)


def _chol_inv_kernel(a_ref, linv_ref, work, lt, dblk):
    n = a_ref.shape[0]
    nb = n // BLK
    work[...] = a_ref[...]
    linv_ref[...] = jnp.zeros_like(linv_ref)
    for k in range(nb):
        s = k * BLK
        _diag_factor(work[s:s + BLK, s:s + BLK], dblk, linv_ref.at[s:s + BLK, s:s + BLK])
        lt[s:s + BLK, s:s + BLK] = dblk[...]
        if k < nb - 1:
            e = s + BLK
            u = _mm(linv_ref[s:s + BLK, s:s + BLK], work[s:s + BLK, e:])
            lt[s:s + BLK, e:] = u
            work[e:, e:] = work[e:, e:] - _mm(u.T, u)
    for i in range(1, nb):
        s = i * BLK
        li = lt[0:s, s:s + BLK].T
        acc = _mm(li, linv_ref[0:s, 0:s])
        linv_ref[s:s + BLK, 0:s] = -_mm(linv_ref[s:s + BLK, s:s + BLK], acc)


def chol_inv(a):
    n = a.shape[0]
    return pl.pallas_call(
        _chol_inv_kernel,
        out_shape=jax.ShapeDtypeStruct((n, n), jnp.float32),
        in_specs=[pl.BlockSpec(memory_space=pltpu.VMEM)],
        out_specs=pl.BlockSpec(memory_space=pltpu.VMEM),
        scratch_shapes=[
            pltpu.VMEM((n, n), jnp.float32),
            pltpu.VMEM((n, n), jnp.float32),
            pltpu.VMEM((BLK, BLK), jnp.float32),
        ],
        compiler_params=pltpu.CompilerParams(vmem_limit_bytes=60 * 1024 * 1024),
    )(a)


def mm(a, b):
    return jnp.dot(a, b, precision=HIGHEST, preferred_element_type=jnp.float32)


def mm_tn(a, b, precision=HIGHEST):
    return lax.dot_general(
        a, b, (((0,), (0,)), ((), ())), precision=precision, preferred_element_type=jnp.float32
    )


def tiles_to_matrix(x, outer, inner):
    rest = x.shape[1:]
    x = x.reshape((outer, inner, TILE) + rest)
    return jnp.swapaxes(x, 0, 1).reshape((outer * inner * TILE,) + rest)


def local(kernel):
    grid_rows = lax.axis_size("row")
    grid_cols = lax.axis_size("col")
    my_row = lax.axis_index("row")
    my_col = lax.axis_index("col")
    rows_loc, cols_loc = kernel.shape
    lead = PANELS * PANEL
    lead_rt = lead // (TILE * grid_rows)
    lead_ct = lead // (TILE * grid_cols)
    lead_r = lead_rt * TILE
    lead_c = lead_ct * TILE

    row_local = jnp.arange(rows_loc, dtype=jnp.int32)
    row_ids = (row_local // TILE * grid_rows + my_row) * TILE + row_local % TILE
    col_local = jnp.arange(cols_loc, dtype=jnp.int32)
    col_ids = (col_local // TILE * grid_cols + my_col) * TILE + col_local % TILE

    corner = lax.all_gather(kernel[:lead_r, :lead_c], "col", axis=1, tiled=True)
    corner = lax.all_gather(corner, "row", axis=0, tiled=True)
    corner, rows_src, cols_src = lax.optimization_barrier(
        (corner, kernel[:lead_r, :], kernel[:, :lead_c])
    )
    corner = tiles_to_matrix(corner, grid_rows, lead_rt)
    a_lead = tiles_to_matrix(corner.T, grid_cols, lead_ct)

    cols_part = lax.all_gather(cols_src, "col", axis=1, tiled=True)
    x_rows_t = tiles_to_matrix(cols_part.T, grid_cols, lead_ct)

    rows_part = lax.all_gather(rows_src, "row", axis=0, tiled=True)
    y_cols = tiles_to_matrix(rows_part, grid_rows, lead_rt)

    linv = chol_inv(a_lead)
    l0inv = linv[:PANEL, :PANEL]
    l1row = linv[PANEL:, :]

    def factor(panel_t, ids):
        g0 = mm(l0inv, panel_t[:PANEL])
        g1 = mm(l1row, panel_t)
        g1 = jnp.where(ids[None, :] >= PANEL, g1, 0.0)
        return jnp.concatenate([g0, g1], axis=0)

    g_rows = factor(x_rows_t, row_ids)
    g_cols = factor(y_cols, col_ids)

    schur = kernel - mm_tn(g_rows, g_cols, lax.Precision.HIGH)
    keep = (row_ids[:, None] >= lead) & (col_ids[None, :] >= lead)
    trailing = jnp.where(keep, schur, 0.0)
    per_col = lead // grid_cols
    factor_out = lax.dynamic_slice_in_dim(g_rows, my_col * per_col, per_col, 0)
    return (trailing, factor_out)


def solution(mesh):
    return jax.shard_map(
        local,
        mesh=mesh,
        in_specs=(P("row", "col"),),
        out_specs=(P("row", "col"), P("col", "row")),
        check_vma=False,
    )
```

```python
import jax
import jax.numpy as jnp
from jax import lax
from jax.experimental import pallas as pl
from jax.experimental.pallas import tpu as pltpu
from jax.sharding import PartitionSpec as P

PANEL = 512
PANELS = 2
TILE = 32
BLK = 128

HIGHEST = lax.Precision.HIGHEST


def _mm(a, b):
    return jnp.dot(a, b, precision=HIGHEST, preferred_element_type=jnp.float32)


def _diag_factor(d, lt_ref, w_ref):
    sub_all = lax.broadcasted_iota(jnp.int32, (BLK, BLK), 0)
    lane_all = lax.broadcasted_iota(jnp.int32, (BLK, BLK), 1)
    lane_row = lax.broadcasted_iota(jnp.int32, (1, BLK), 1)
    dm = d
    wm = (sub_all == lane_all).astype(jnp.float32)
    part = 8
    for q in range(BLK // part):
        lo = q * part
        rows = BLK - lo
        sub = lax.broadcasted_iota(jnp.int32, (rows, BLK), 0) + lo
        lane = lax.broadcasted_iota(jnp.int32, (rows, BLK), 1)

        def step(j, carry, sub=sub, lane=lane):
            dq, wq = carry
            rowsel = sub == j
            rowj = jnp.sum(jnp.where(rowsel, dq, 0.0), axis=0, keepdims=True)
            colj = jnp.sum(jnp.where(lane == j, dq, 0.0), axis=1, keepdims=True)
            piv = jnp.sum(jnp.where(lane_row == j, rowj, 0.0), axis=1, keepdims=True)
            inv = lax.rsqrt(piv)
            lrow = jnp.where(lane_row >= j, rowj * inv, 0.0)
            lcol = jnp.where(sub[:, 0:1] > j, colj * inv, 0.0)
            dq = dq - lcol * lrow
            wj = jnp.sum(jnp.where(rowsel, wq, 0.0), axis=0, keepdims=True) * inv
            wq = jnp.where(rowsel, wj, wq - lcol * wj)
            lt_ref[pl.ds(j, 1), :] = lrow
            return dq, wq

        dq, wq = lax.fori_loop(lo, lo + part, step, (dm[lo:], wm[lo:]))
        w_ref[lo:lo + part, :] = wq[:part]
        if q + 1 < BLK // part:
            dm = jnp.concatenate([jnp.zeros((lo + part, BLK), jnp.float32), dq[part:]], axis=0)
            wm = jnp.concatenate([jnp.zeros((lo + part, BLK), jnp.float32), wq[part:]], axis=0)


def _chol_inv_kernel(a_ref, linv_ref, work, lt, dblk):
    n = a_ref.shape[0]
    nb = n // BLK
    work[...] = a_ref[...]
    linv_ref[...] = jnp.zeros_like(linv_ref)
    for k in range(nb):
        s = k * BLK
        _diag_factor(work[s:s + BLK, s:s + BLK], dblk, linv_ref.at[s:s + BLK, s:s + BLK])
        lt[s:s + BLK, s:s + BLK] = dblk[...]
        if k < nb - 1:
            e = s + BLK
            u = _mm(linv_ref[s:s + BLK, s:s + BLK], work[s:s + BLK, e:])
            lt[s:s + BLK, e:] = u
            work[e:, e:] = work[e:, e:] - _mm(u.T, u)
    for i in range(1, nb):
        s = i * BLK
        li = lt[0:s, s:s + BLK].T
        acc = _mm(li, linv_ref[0:s, 0:s])
        linv_ref[s:s + BLK, 0:s] = -_mm(linv_ref[s:s + BLK, s:s + BLK], acc)


def chol_inv(a):
    n = a.shape[0]
    return pl.pallas_call(
        _chol_inv_kernel,
        out_shape=jax.ShapeDtypeStruct((n, n), jnp.float32),
        in_specs=[pl.BlockSpec(memory_space=pltpu.VMEM)],
        out_specs=pl.BlockSpec(memory_space=pltpu.VMEM),
        scratch_shapes=[
            pltpu.VMEM((n, n), jnp.float32),
            pltpu.VMEM((n, n), jnp.float32),
            pltpu.VMEM((BLK, BLK), jnp.float32),
        ],
        compiler_params=pltpu.CompilerParams(vmem_limit_bytes=60 * 1024 * 1024),
    )(a)


def mm(a, b):
    return jnp.dot(a, b, precision=HIGHEST, preferred_element_type=jnp.float32)


def mm_tn(a, b, precision=HIGHEST):
    return lax.dot_general(
        a, b, (((0,), (0,)), ((), ())), precision=precision, preferred_element_type=jnp.float32
    )


def tiles_to_matrix(x, outer, inner):
    rest = x.shape[1:]
    x = x.reshape((outer, inner, TILE) + rest)
    return jnp.swapaxes(x, 0, 1).reshape((outer * inner * TILE,) + rest)


def local(kernel):
    grid_rows = lax.axis_size("row")
    grid_cols = lax.axis_size("col")
    my_row = lax.axis_index("row")
    my_col = lax.axis_index("col")
    rows_loc, cols_loc = kernel.shape
    lead = PANELS * PANEL
    lead_rt = lead // (TILE * grid_rows)
    lead_ct = lead // (TILE * grid_cols)
    lead_r = lead_rt * TILE
    lead_c = lead_ct * TILE

    row_local = jnp.arange(rows_loc, dtype=jnp.int32)
    row_ids = (row_local // TILE * grid_rows + my_row) * TILE + row_local % TILE
    col_local = jnp.arange(cols_loc, dtype=jnp.int32)
    col_ids = (col_local // TILE * grid_cols + my_col) * TILE + col_local % TILE

    piece = kernel[:lead_r, :lead_c].reshape(lead_r, lead_ct, TILE).transpose(1, 0, 2)
    piece = lax.all_gather(piece, "col", axis=2, tiled=True)
    corner = piece.transpose(1, 0, 2).reshape(lead_r, lead)
    corner = lax.all_gather(corner, "row", axis=0, tiled=True)
    corner, rows_src, cols_src = lax.optimization_barrier(
        (corner, kernel[:lead_r, :], kernel[:, :lead_c])
    )
    a_lead = tiles_to_matrix(corner, grid_rows, lead_rt)

    cols_part = lax.all_gather(cols_src, "col", axis=1, tiled=True)
    x_rows_t = tiles_to_matrix(cols_part.T, grid_cols, lead_ct)

    rows_part = lax.all_gather(rows_src, "row", axis=0, tiled=True)
    y_cols = tiles_to_matrix(rows_part, grid_rows, lead_rt)

    linv = chol_inv(a_lead)
    l0inv = linv[:PANEL, :PANEL]
    l1row = linv[PANEL:, :]

    def factor(panel_t, ids):
        g0 = mm(l0inv, panel_t[:PANEL])
        g1 = mm(l1row, panel_t)
        g1 = jnp.where(ids[None, :] >= PANEL, g1, 0.0)
        return jnp.concatenate([g0, g1], axis=0)

    g_rows = factor(x_rows_t, row_ids)
    g_cols = factor(y_cols, col_ids)

    schur = kernel - mm_tn(g_rows, g_cols, lax.Precision.HIGH)
    keep = (row_ids[:, None] >= lead) & (col_ids[None, :] >= lead)
    trailing = jnp.where(keep, schur, 0.0)
    per_col = lead // grid_cols
    factor_out = lax.dynamic_slice_in_dim(g_rows, my_col * per_col, per_col, 0)
    return (trailing, factor_out)


def solution(mesh):
    return jax.shard_map(
        local,
        mesh=mesh,
        in_specs=(P("row", "col"),),
        out_specs=(P("row", "col"), P("col", "row")),
        check_vma=False,
    )
```

```python
import functools
import jax
import jax.numpy as jnp
from jax import lax
from jax.experimental import pallas as pl
from jax.experimental.pallas import tpu as pltpu
from jax.sharding import PartitionSpec as P

PANEL = 512
PANELS = 2
TILE = 32
BLK = 128

HIGHEST = lax.Precision.HIGHEST
MESH = pl.DeviceIdType.MESH


def _col_gather_kernel(n, x_ref, o_ref, send_sems, recv_sems):
    me = lax.axis_index("col")
    row = lax.axis_index("row")
    barrier = pltpu.get_barrier_semaphore()
    for p in range(1, n):
        peer = lax.rem(me + p, n)
        pl.semaphore_signal(barrier, inc=1, device_id=(row, peer), device_id_type=MESH)
    pl.semaphore_wait(barrier, n - 1)
    copies = []
    for p in range(1, n):
        peer = lax.rem(me + p, n)
        cp = pltpu.make_async_remote_copy(
            src_ref=x_ref,
            dst_ref=o_ref.at[me],
            send_sem=send_sems.at[p - 1],
            recv_sem=recv_sems.at[p - 1],
            device_id=(row, peer),
            device_id_type=MESH,
        )
        cp.start()
        copies.append(cp)
    o_ref[me] = x_ref[...]
    for cp in copies:
        cp.wait()


def col_gather(x, n):
    return pl.pallas_call(
        functools.partial(_col_gather_kernel, n),
        out_shape=jax.ShapeDtypeStruct((n,) + x.shape, x.dtype),
        in_specs=[pl.BlockSpec(memory_space=pltpu.VMEM)],
        out_specs=pl.BlockSpec(memory_space=pltpu.VMEM),
        scratch_shapes=[pltpu.SemaphoreType.DMA((n - 1,)), pltpu.SemaphoreType.DMA((n - 1,))],
        compiler_params=pltpu.CompilerParams(collective_id=0, has_side_effects=True),
    )(x)


def _mm(a, b):
    return jnp.dot(a, b, precision=HIGHEST, preferred_element_type=jnp.float32)


def _diag_factor(d, lt_ref, w_ref):
    sub_all = lax.broadcasted_iota(jnp.int32, (BLK, BLK), 0)
    lane_all = lax.broadcasted_iota(jnp.int32, (BLK, BLK), 1)
    lane_row = lax.broadcasted_iota(jnp.int32, (1, BLK), 1)
    dm = d
    wm = (sub_all == lane_all).astype(jnp.float32)
    part = 8
    for q in range(BLK // part):
        lo = q * part
        rows = BLK - lo
        sub = lax.broadcasted_iota(jnp.int32, (rows, BLK), 0) + lo
        lane = lax.broadcasted_iota(jnp.int32, (rows, BLK), 1)

        def step(j, carry, sub=sub, lane=lane):
            dq, wq = carry
            rowsel = sub == j
            rowj = jnp.sum(jnp.where(rowsel, dq, 0.0), axis=0, keepdims=True)
            colj = jnp.sum(jnp.where(lane == j, dq, 0.0), axis=1, keepdims=True)
            piv = jnp.sum(jnp.where(lane_row == j, rowj, 0.0), axis=1, keepdims=True)
            inv = lax.rsqrt(piv)
            lrow = jnp.where(lane_row >= j, rowj * inv, 0.0)
            lcol = jnp.where(sub[:, 0:1] > j, colj * inv, 0.0)
            dq = dq - lcol * lrow
            wj = jnp.sum(jnp.where(rowsel, wq, 0.0), axis=0, keepdims=True) * inv
            wq = jnp.where(rowsel, wj, wq - lcol * wj)
            lt_ref[pl.ds(j, 1), :] = lrow
            return dq, wq

        dq, wq = lax.fori_loop(lo, lo + part, step, (dm[lo:], wm[lo:]))
        w_ref[lo:lo + part, :] = wq[:part]
        if q + 1 < BLK // part:
            dm = jnp.concatenate([jnp.zeros((lo + part, BLK), jnp.float32), dq[part:]], axis=0)
            wm = jnp.concatenate([jnp.zeros((lo + part, BLK), jnp.float32), wq[part:]], axis=0)


def _chol_inv_kernel(a_ref, linv_ref, work, lt, dblk):
    n = a_ref.shape[0]
    nb = n // BLK
    work[...] = a_ref[...]
    linv_ref[...] = jnp.zeros_like(linv_ref)
    for k in range(nb):
        s = k * BLK
        _diag_factor(work[s:s + BLK, s:s + BLK], dblk, linv_ref.at[s:s + BLK, s:s + BLK])
        lt[s:s + BLK, s:s + BLK] = dblk[...]
        if k < nb - 1:
            e = s + BLK
            u = _mm(linv_ref[s:s + BLK, s:s + BLK], work[s:s + BLK, e:])
            lt[s:s + BLK, e:] = u
            work[e:, e:] = work[e:, e:] - _mm(u.T, u)
    for i in range(1, nb):
        s = i * BLK
        li = lt[0:s, s:s + BLK].T
        acc = _mm(li, linv_ref[0:s, 0:s])
        linv_ref[s:s + BLK, 0:s] = -_mm(linv_ref[s:s + BLK, s:s + BLK], acc)


def chol_inv(a):
    n = a.shape[0]
    return pl.pallas_call(
        _chol_inv_kernel,
        out_shape=jax.ShapeDtypeStruct((n, n), jnp.float32),
        in_specs=[pl.BlockSpec(memory_space=pltpu.VMEM)],
        out_specs=pl.BlockSpec(memory_space=pltpu.VMEM),
        scratch_shapes=[
            pltpu.VMEM((n, n), jnp.float32),
            pltpu.VMEM((n, n), jnp.float32),
            pltpu.VMEM((BLK, BLK), jnp.float32),
        ],
        compiler_params=pltpu.CompilerParams(vmem_limit_bytes=60 * 1024 * 1024),
    )(a)


def mm(a, b):
    return jnp.dot(a, b, precision=HIGHEST, preferred_element_type=jnp.float32)


def mm_tn(a, b, precision=HIGHEST):
    return lax.dot_general(
        a, b, (((0,), (0,)), ((), ())), precision=precision, preferred_element_type=jnp.float32
    )


def tiles_to_matrix(x, outer, inner):
    rest = x.shape[1:]
    x = x.reshape((outer, inner, TILE) + rest)
    return jnp.swapaxes(x, 0, 1).reshape((outer * inner * TILE,) + rest)


def local(kernel):
    grid_rows = lax.axis_size("row")
    grid_cols = lax.axis_size("col")
    my_row = lax.axis_index("row")
    my_col = lax.axis_index("col")
    rows_loc, cols_loc = kernel.shape
    lead = PANELS * PANEL
    lead_rt = lead // (TILE * grid_rows)
    lead_ct = lead // (TILE * grid_cols)
    lead_r = lead_rt * TILE
    lead_c = lead_ct * TILE

    row_local = jnp.arange(rows_loc, dtype=jnp.int32)
    row_ids = (row_local // TILE * grid_rows + my_row) * TILE + row_local % TILE
    col_local = jnp.arange(cols_loc, dtype=jnp.int32)
    col_ids = (col_local // TILE * grid_cols + my_col) * TILE + col_local % TILE

    piece = col_gather(kernel[:lead_r, :lead_c], grid_cols)
    piece = piece.reshape(grid_cols, lead_r, lead_ct, TILE).transpose(1, 2, 0, 3)
    corner = piece.reshape(lead_r, lead)
    corner = lax.all_gather(corner, "row", axis=0, tiled=True)
    corner, rows_src, cols_src = lax.optimization_barrier(
        (corner, kernel[:lead_r, :], kernel[:, :lead_c])
    )
    a_lead = tiles_to_matrix(corner, grid_rows, lead_rt)

    cols_part = lax.all_gather(cols_src, "col", axis=1, tiled=True)
    x_rows_t = tiles_to_matrix(cols_part.T, grid_cols, lead_ct)

    rows_part = lax.all_gather(rows_src, "row", axis=0, tiled=True)
    y_cols = tiles_to_matrix(rows_part, grid_rows, lead_rt)

    linv = chol_inv(a_lead)
    l0inv = linv[:PANEL, :PANEL]
    l1row = linv[PANEL:, :]

    def factor(panel_t, ids):
        g0 = mm(l0inv, panel_t[:PANEL])
        g1 = mm(l1row, panel_t)
        g1 = jnp.where(ids[None, :] >= PANEL, g1, 0.0)
        return jnp.concatenate([g0, g1], axis=0)

    g_rows = factor(x_rows_t, row_ids)
    g_cols = factor(y_cols, col_ids)

    schur = kernel - mm_tn(g_rows, g_cols, lax.Precision.HIGH)
    keep = (row_ids[:, None] >= lead) & (col_ids[None, :] >= lead)
    trailing = jnp.where(keep, schur, 0.0)
    per_col = lead // grid_cols
    factor_out = lax.dynamic_slice_in_dim(g_rows, my_col * per_col, per_col, 0)
    return (trailing, factor_out)


def solution(mesh):
    return jax.shard_map(
        local,
        mesh=mesh,
        in_specs=(P("row", "col"),),
        out_specs=(P("row", "col"), P("col", "row")),
        check_vma=False,
    )
```

```python
import jax
import jax.numpy as jnp
from jax import lax
from jax.experimental import pallas as pl
from jax.experimental.pallas import tpu as pltpu
from jax.sharding import PartitionSpec as P

PANEL = 512
PANELS = 2
TILE = 32
BLK = 128

HIGHEST = lax.Precision.HIGHEST


def _mm(a, b):
    return jnp.dot(a, b, precision=HIGHEST, preferred_element_type=jnp.float32)


def _diag_factor(d, lt_ref, w_ref):
    sub_all = lax.broadcasted_iota(jnp.int32, (BLK, BLK), 0)
    lane_all = lax.broadcasted_iota(jnp.int32, (BLK, BLK), 1)
    lane_row = lax.broadcasted_iota(jnp.int32, (1, BLK), 1)
    dm = d
    wm = (sub_all == lane_all).astype(jnp.float32)
    part = 8
    for q in range(BLK // part):
        lo = q * part
        rows = BLK - lo
        sub = lax.broadcasted_iota(jnp.int32, (rows, BLK), 0) + lo
        lane = lax.broadcasted_iota(jnp.int32, (rows, BLK), 1)

        def step(t, carry, sub=sub, lane=lane, lo=lo):
            dq, wq = carry
            j = lo + 2 * t
            sel0 = sub == j
            sel1 = sub == j + 1
            r0 = jnp.sum(jnp.where(sel0, dq, 0.0), axis=0, keepdims=True)
            r1 = jnp.sum(jnp.where(sel1, dq, 0.0), axis=0, keepdims=True)
            c0 = jnp.sum(jnp.where(lane == j, dq, 0.0), axis=1, keepdims=True)
            c1 = jnp.sum(jnp.where(lane == j + 1, dq, 0.0), axis=1, keepdims=True)
            a = jnp.sum(jnp.where(lane_row == j, r0, 0.0), axis=1, keepdims=True)
            b = jnp.sum(jnp.where(lane_row == j + 1, r0, 0.0), axis=1, keepdims=True)
            d = jnp.sum(jnp.where(lane_row == j + 1, r1, 0.0), axis=1, keepdims=True)
            i1 = lax.rsqrt(a)
            l21 = b * i1
            i2 = lax.rsqrt(d - l21 * l21)
            lrow0 = jnp.where(lane_row >= j, r0 * i1, 0.0)
            lrow1 = jnp.where(lane_row >= j + 1, (r1 - l21 * lrow0) * i2, 0.0)
            lcol0 = jnp.where(sub[:, 0:1] > j, c0 * i1, 0.0)
            lcol1 = jnp.where(sub[:, 0:1] > j + 1, (c1 - l21 * lcol0) * i2, 0.0)
            dq = dq - lcol0 * lrow0 - lcol1 * lrow1
            w0 = jnp.sum(jnp.where(sel0, wq, 0.0), axis=0, keepdims=True)
            w1 = jnp.sum(jnp.where(sel1, wq, 0.0), axis=0, keepdims=True)
            wj0 = w0 * i1
            wj1 = (w1 - l21 * wj0) * i2
            wq = wq - lcol0 * wj0 - lcol1 * wj1
            wq = jnp.where(sel0, wj0, jnp.where(sel1, wj1, wq))
            lt_ref[pl.ds(j, 1), :] = lrow0
            lt_ref[pl.ds(j + 1, 1), :] = lrow1
            return dq, wq

        dq, wq = lax.fori_loop(0, part // 2, step, (dm[lo:], wm[lo:]))
        w_ref[lo:lo + part, :] = wq[:part]
        if q + 1 < BLK // part:
            dm = jnp.concatenate([jnp.zeros((lo + part, BLK), jnp.float32), dq[part:]], axis=0)
            wm = jnp.concatenate([jnp.zeros((lo + part, BLK), jnp.float32), wq[part:]], axis=0)


def _chol_inv_kernel(a_ref, linv_ref, work, lt, dblk):
    n = a_ref.shape[0]
    nb = n // BLK
    work[...] = a_ref[...]
    linv_ref[...] = jnp.zeros_like(linv_ref)
    for k in range(nb):
        s = k * BLK
        _diag_factor(work[s:s + BLK, s:s + BLK], dblk, linv_ref.at[s:s + BLK, s:s + BLK])
        lt[s:s + BLK, s:s + BLK] = dblk[...]
        if k < nb - 1:
            e = s + BLK
            u = _mm(linv_ref[s:s + BLK, s:s + BLK], work[s:s + BLK, e:])
            lt[s:s + BLK, e:] = u
            work[e:, e:] = work[e:, e:] - _mm(u.T, u)
    for i in range(1, nb):
        s = i * BLK
        li = lt[0:s, s:s + BLK].T
        acc = _mm(li, linv_ref[0:s, 0:s])
        linv_ref[s:s + BLK, 0:s] = -_mm(linv_ref[s:s + BLK, s:s + BLK], acc)


def chol_inv(a):
    n = a.shape[0]
    return pl.pallas_call(
        _chol_inv_kernel,
        out_shape=jax.ShapeDtypeStruct((n, n), jnp.float32),
        in_specs=[pl.BlockSpec(memory_space=pltpu.VMEM)],
        out_specs=pl.BlockSpec(memory_space=pltpu.VMEM),
        scratch_shapes=[
            pltpu.VMEM((n, n), jnp.float32),
            pltpu.VMEM((n, n), jnp.float32),
            pltpu.VMEM((BLK, BLK), jnp.float32),
        ],
        compiler_params=pltpu.CompilerParams(vmem_limit_bytes=60 * 1024 * 1024),
    )(a)


def mm(a, b):
    return jnp.dot(a, b, precision=HIGHEST, preferred_element_type=jnp.float32)


def mm_tn(a, b, precision=HIGHEST):
    return lax.dot_general(
        a, b, (((0,), (0,)), ((), ())), precision=precision, preferred_element_type=jnp.float32
    )


def tiles_to_matrix(x, outer, inner):
    rest = x.shape[1:]
    x = x.reshape((outer, inner, TILE) + rest)
    return jnp.swapaxes(x, 0, 1).reshape((outer * inner * TILE,) + rest)


def local(kernel):
    grid_rows = lax.axis_size("row")
    grid_cols = lax.axis_size("col")
    my_row = lax.axis_index("row")
    my_col = lax.axis_index("col")
    rows_loc, cols_loc = kernel.shape
    lead = PANELS * PANEL
    lead_rt = lead // (TILE * grid_rows)
    lead_ct = lead // (TILE * grid_cols)
    lead_r = lead_rt * TILE
    lead_c = lead_ct * TILE

    row_local = jnp.arange(rows_loc, dtype=jnp.int32)
    row_ids = (row_local // TILE * grid_rows + my_row) * TILE + row_local % TILE
    col_local = jnp.arange(cols_loc, dtype=jnp.int32)
    col_ids = (col_local // TILE * grid_cols + my_col) * TILE + col_local % TILE

    piece = kernel[:lead_r, :lead_c].reshape(lead_r, lead_ct, TILE).transpose(1, 0, 2)
    piece = lax.all_gather(piece, "col", axis=2, tiled=True)
    corner = piece.transpose(1, 0, 2).reshape(lead_r, lead)
    corner = lax.all_gather(corner, "row", axis=0, tiled=True)
    corner, rows_src, cols_src = lax.optimization_barrier(
        (corner, kernel[:lead_r, :], kernel[:, :lead_c])
    )
    a_lead = tiles_to_matrix(corner, grid_rows, lead_rt)

    cols_part = lax.all_gather(cols_src, "col", axis=1, tiled=True)
    x_rows_t = tiles_to_matrix(cols_part.T, grid_cols, lead_ct)

    rows_part = lax.all_gather(rows_src, "row", axis=0, tiled=True)
    y_cols = tiles_to_matrix(rows_part, grid_rows, lead_rt)

    linv = chol_inv(a_lead)
    l0inv = linv[:PANEL, :PANEL]
    l1row = linv[PANEL:, :]

    def factor(panel_t, ids):
        g0 = mm(l0inv, panel_t[:PANEL])
        g1 = mm(l1row, panel_t)
        g1 = jnp.where(ids[None, :] >= PANEL, g1, 0.0)
        return jnp.concatenate([g0, g1], axis=0)

    g_rows = factor(x_rows_t, row_ids)
    g_cols = factor(y_cols, col_ids)

    schur = kernel - mm_tn(g_rows, g_cols, lax.Precision.HIGH)
    keep = (row_ids[:, None] >= lead) & (col_ids[None, :] >= lead)
    trailing = jnp.where(keep, schur, 0.0)
    per_col = lead // grid_cols
    factor_out = lax.dynamic_slice_in_dim(g_rows, my_col * per_col, per_col, 0)
    return (trailing, factor_out)


def solution(mesh):
    return jax.shard_map(
        local,
        mesh=mesh,
        in_specs=(P("row", "col"),),
        out_specs=(P("row", "col"), P("col", "row")),
        check_vma=False,
    )
```

```python
import jax
import jax.numpy as jnp
from jax import lax
from jax.experimental import pallas as pl
from jax.experimental.pallas import tpu as pltpu
from jax.sharding import PartitionSpec as P

PANEL = 512
PANELS = 2
TILE = 32
BLK = 128
KCOL = 8

HIGHEST = lax.Precision.HIGHEST


def _mm(a, b):
    return jnp.dot(a, b, precision=HIGHEST, preferred_element_type=jnp.float32)


def _diag_factor(d, lt_ref, w_ref):
    sub_all = lax.broadcasted_iota(jnp.int32, (BLK, BLK), 0)
    lane_all = lax.broadcasted_iota(jnp.int32, (BLK, BLK), 1)
    lane_row = lax.broadcasted_iota(jnp.int32, (1, BLK), 1)
    dm = d
    wm = (sub_all == lane_all).astype(jnp.float32)
    part = 8
    for q in range(BLK // part):
        lo = q * part
        rows = BLK - lo
        sub = lax.broadcasted_iota(jnp.int32, (rows, BLK), 0) + lo
        lane = lax.broadcasted_iota(jnp.int32, (rows, BLK), 1)

        def step(t, carry, sub=sub, lane=lane, lo=lo):
            dq, wq = carry
            j = lo + KCOL * t
            sels = [sub == j + m for m in range(KCOL)]
            rr = [jnp.sum(jnp.where(s, dq, 0.0), axis=0, keepdims=True) for s in sels]
            cc = [jnp.sum(jnp.where(lane == j + m, dq, 0.0), axis=1, keepdims=True) for m in range(KCOL)]
            wr = [jnp.sum(jnp.where(s, wq, 0.0), axis=0, keepdims=True) for s in sels]
            lk = [[None] * KCOL for _ in range(KCOL)]
            inv = [None] * KCOL
            for m in range(KCOL):
                for p in range(m + 1):
                    v = jnp.sum(jnp.where(lane_row == j + p, rr[m], 0.0), axis=1, keepdims=True)
                    for q in range(p):
                        v = v - lk[m][q] * lk[p][q]
                    if p < m:
                        lk[m][p] = v * inv[p]
                    else:
                        inv[m] = lax.rsqrt(v)
            lrow, lcol, wj = [], [], []
            for m in range(KCOL):
                rv, cv, wv = rr[m], cc[m], wr[m]
                for p in range(m):
                    rv = rv - lk[m][p] * lrow[p]
                    cv = cv - lk[m][p] * lcol[p]
                    wv = wv - lk[m][p] * wj[p]
                lrow.append(jnp.where(lane_row >= j + m, rv * inv[m], 0.0))
                lcol.append(jnp.where(sub[:, 0:1] > j + m, cv * inv[m], 0.0))
                wj.append(wv * inv[m])
            for m in range(KCOL):
                dq = dq - lcol[m] * lrow[m]
                wq = wq - lcol[m] * wj[m]
            for m in range(KCOL):
                wq = jnp.where(sels[m], wj[m], wq)
                lt_ref[pl.ds(j + m, 1), :] = lrow[m]
            return dq, wq

        dq, wq = lax.fori_loop(0, part // KCOL, step, (dm[lo:], wm[lo:]))
        w_ref[lo:lo + part, :] = wq[:part]
        if q + 1 < BLK // part:
            dm = jnp.concatenate([jnp.zeros((lo + part, BLK), jnp.float32), dq[part:]], axis=0)
            wm = jnp.concatenate([jnp.zeros((lo + part, BLK), jnp.float32), wq[part:]], axis=0)


def _chol_inv_kernel(a_ref, linv_ref, work, lt, dblk):
    n = a_ref.shape[0]
    nb = n // BLK
    work[...] = a_ref[...]
    linv_ref[...] = jnp.zeros_like(linv_ref)
    for k in range(nb):
        s = k * BLK
        _diag_factor(work[s:s + BLK, s:s + BLK], dblk, linv_ref.at[s:s + BLK, s:s + BLK])
        lt[s:s + BLK, s:s + BLK] = dblk[...]
        if k < nb - 1:
            e = s + BLK
            u = _mm(linv_ref[s:s + BLK, s:s + BLK], work[s:s + BLK, e:])
            lt[s:s + BLK, e:] = u
            work[e:, e:] = work[e:, e:] - _mm(u.T, u)
    for i in range(1, nb):
        s = i * BLK
        li = lt[0:s, s:s + BLK].T
        acc = _mm(li, linv_ref[0:s, 0:s])
        linv_ref[s:s + BLK, 0:s] = -_mm(linv_ref[s:s + BLK, s:s + BLK], acc)


def chol_inv(a):
    n = a.shape[0]
    return pl.pallas_call(
        _chol_inv_kernel,
        out_shape=jax.ShapeDtypeStruct((n, n), jnp.float32),
        in_specs=[pl.BlockSpec(memory_space=pltpu.VMEM)],
        out_specs=pl.BlockSpec(memory_space=pltpu.VMEM),
        scratch_shapes=[
            pltpu.VMEM((n, n), jnp.float32),
            pltpu.VMEM((n, n), jnp.float32),
            pltpu.VMEM((BLK, BLK), jnp.float32),
        ],
        compiler_params=pltpu.CompilerParams(vmem_limit_bytes=60 * 1024 * 1024),
    )(a)


def mm(a, b):
    return jnp.dot(a, b, precision=HIGHEST, preferred_element_type=jnp.float32)


def mm_tn(a, b, precision=HIGHEST):
    return lax.dot_general(
        a, b, (((0,), (0,)), ((), ())), precision=precision, preferred_element_type=jnp.float32
    )


def tiles_to_matrix(x, outer, inner):
    rest = x.shape[1:]
    x = x.reshape((outer, inner, TILE) + rest)
    return jnp.swapaxes(x, 0, 1).reshape((outer * inner * TILE,) + rest)


def local(kernel):
    grid_rows = lax.axis_size("row")
    grid_cols = lax.axis_size("col")
    my_row = lax.axis_index("row")
    my_col = lax.axis_index("col")
    rows_loc, cols_loc = kernel.shape
    lead = PANELS * PANEL
    lead_rt = lead // (TILE * grid_rows)
    lead_ct = lead // (TILE * grid_cols)
    lead_r = lead_rt * TILE
    lead_c = lead_ct * TILE

    row_local = jnp.arange(rows_loc, dtype=jnp.int32)
    row_ids = (row_local // TILE * grid_rows + my_row) * TILE + row_local % TILE
    col_local = jnp.arange(cols_loc, dtype=jnp.int32)
    col_ids = (col_local // TILE * grid_cols + my_col) * TILE + col_local % TILE

    piece = kernel[:lead_r, :lead_c].reshape(lead_r, lead_ct, TILE).transpose(1, 0, 2)
    piece = lax.all_gather(piece, "col", axis=2, tiled=True)
    corner = piece.transpose(1, 0, 2).reshape(lead_r, lead)
    corner = lax.all_gather(corner, "row", axis=0, tiled=True)
    corner, rows_src, cols_src = lax.optimization_barrier(
        (corner, kernel[:lead_r, :], kernel[:, :lead_c])
    )
    a_lead = tiles_to_matrix(corner, grid_rows, lead_rt)

    cols_part = lax.all_gather(cols_src, "col", axis=1, tiled=True)
    x_rows_t = tiles_to_matrix(cols_part.T, grid_cols, lead_ct)

    rows_part = lax.all_gather(rows_src, "row", axis=0, tiled=True)
    y_cols = tiles_to_matrix(rows_part, grid_rows, lead_rt)

    linv = chol_inv(a_lead)
    l0inv = linv[:PANEL, :PANEL]
    l1row = linv[PANEL:, :]

    def factor(panel_t, ids):
        g0 = mm(l0inv, panel_t[:PANEL])
        g1 = mm(l1row, panel_t)
        g1 = jnp.where(ids[None, :] >= PANEL, g1, 0.0)
        return jnp.concatenate([g0, g1], axis=0)

    g_rows = factor(x_rows_t, row_ids)
    g_cols = factor(y_cols, col_ids)

    schur = kernel - mm_tn(g_rows, g_cols, lax.Precision.HIGH)
    keep = (row_ids[:, None] >= lead) & (col_ids[None, :] >= lead)
    trailing = jnp.where(keep, schur, 0.0)
    per_col = lead // grid_cols
    factor_out = lax.dynamic_slice_in_dim(g_rows, my_col * per_col, per_col, 0)
    return (trailing, factor_out)


def solution(mesh):
    return jax.shard_map(
        local,
        mesh=mesh,
        in_specs=(P("row", "col"),),
        out_specs=(P("row", "col"), P("col", "row")),
        check_vma=False,
    )
```

```python
import jax
import jax.numpy as jnp
from jax import lax
from jax.experimental import pallas as pl
from jax.experimental.pallas import tpu as pltpu
from jax.sharding import PartitionSpec as P

PANEL = 512
PANELS = 2
TILE = 32
BLK = 128
KCOL = 8

HIGHEST = lax.Precision.HIGHEST


def _mm(a, b):
    return jnp.dot(a, b, precision=HIGHEST, preferred_element_type=jnp.float32)


def _diag_factor(d, lt_ref, w_ref):
    sub_all = lax.broadcasted_iota(jnp.int32, (BLK, BLK), 0)
    lane_all = lax.broadcasted_iota(jnp.int32, (BLK, BLK), 1)
    lane_row = lax.broadcasted_iota(jnp.int32, (1, BLK), 1)
    dm = d
    wm = (sub_all == lane_all).astype(jnp.float32)
    part = 8
    for q in range(BLK // part):
        lo = q * part
        rows = BLK - lo
        sub = lax.broadcasted_iota(jnp.int32, (rows, BLK), 0) + lo
        lane = lax.broadcasted_iota(jnp.int32, (rows, BLK), 1)

        def step(t, carry, sub=sub, lane=lane, lo=lo):
            dq, wq = carry
            j = lo + KCOL * t
            sels = [sub == j + m for m in range(KCOL)]
            rr = [jnp.sum(jnp.where(s, dq, 0.0), axis=0, keepdims=True) for s in sels]
            cc = [jnp.sum(jnp.where(lane == j + m, dq, 0.0), axis=1, keepdims=True) for m in range(KCOL)]
            wr = [jnp.sum(jnp.where(s, wq, 0.0), axis=0, keepdims=True) for s in sels]
            lk = [[None] * KCOL for _ in range(KCOL)]
            inv = [None] * KCOL
            for m in range(KCOL):
                for p in range(m + 1):
                    v = jnp.sum(jnp.where(lane_row == j + p, rr[m], 0.0), axis=1, keepdims=True)
                    for q in range(p):
                        v = v - lk[m][q] * lk[p][q]
                    if p < m:
                        lk[m][p] = v * inv[p]
                    else:
                        inv[m] = lax.rsqrt(v)
            lrow, lcol, wj = [], [], []
            for m in range(KCOL):
                rv, cv, wv = rr[m], cc[m], wr[m]
                for p in range(m):
                    rv = rv - lk[m][p] * lrow[p]
                    cv = cv - lk[m][p] * lcol[p]
                    wv = wv - lk[m][p] * wj[p]
                lrow.append(jnp.where(lane_row >= j + m, rv * inv[m], 0.0))
                lcol.append(jnp.where(sub[:, 0:1] > j + m, cv * inv[m], 0.0))
                wj.append(wv * inv[m])
            for m in range(KCOL):
                dq = dq - lcol[m] * lrow[m]
                wq = wq - lcol[m] * wj[m]
            for m in range(KCOL):
                wq = jnp.where(sels[m], wj[m], wq)
                lt_ref[pl.ds(j + m, 1), :] = lrow[m]
            return dq, wq

        dq, wq = lax.fori_loop(0, part // KCOL, step, (dm[lo:], wm[lo:]))
        w_ref[lo:lo + part, :] = wq[:part]
        if q + 1 < BLK // part:
            dm = jnp.concatenate([jnp.zeros((lo + part, BLK), jnp.float32), dq[part:]], axis=0)
            wm = jnp.concatenate([jnp.zeros((lo + part, BLK), jnp.float32), wq[part:]], axis=0)


def _chol_inv_kernel(a_ref, linv_ref, work, lt, dblk):
    n = a_ref.shape[0]
    nb = n // BLK
    work[...] = a_ref[...]
    linv_ref[...] = jnp.zeros_like(linv_ref)
    for k in range(nb):
        s = k * BLK
        _diag_factor(work[s:s + BLK, s:s + BLK], dblk, linv_ref.at[s:s + BLK, s:s + BLK])
        lt[s:s + BLK, s:s + BLK] = dblk[...]
        if k < nb - 1:
            e = s + BLK
            u = _mm(linv_ref[s:s + BLK, s:s + BLK], work[s:s + BLK, e:])
            lt[s:s + BLK, e:] = u
            work[e:, e:] = work[e:, e:] - _mm(u.T, u)
    for i in range(1, nb):
        s = i * BLK
        li = lt[0:s, s:s + BLK].T
        acc = _mm(li, linv_ref[0:s, 0:s])
        linv_ref[s:s + BLK, 0:s] = -_mm(linv_ref[s:s + BLK, s:s + BLK], acc)


def chol_inv(a):
    n = a.shape[0]
    return pl.pallas_call(
        _chol_inv_kernel,
        out_shape=jax.ShapeDtypeStruct((n, n), jnp.float32),
        in_specs=[pl.BlockSpec(memory_space=pltpu.VMEM)],
        out_specs=pl.BlockSpec(memory_space=pltpu.VMEM),
        scratch_shapes=[
            pltpu.VMEM((n, n), jnp.float32),
            pltpu.VMEM((n, n), jnp.float32),
            pltpu.VMEM((BLK, BLK), jnp.float32),
        ],
        compiler_params=pltpu.CompilerParams(vmem_limit_bytes=60 * 1024 * 1024),
    )(a)


def mm(a, b):
    return jnp.dot(a, b, precision=HIGHEST, preferred_element_type=jnp.float32)


def mm_tn(a, b, precision=HIGHEST):
    return lax.dot_general(
        a, b, (((0,), (0,)), ((), ())), precision=precision, preferred_element_type=jnp.float32
    )


def tiles_to_matrix(x, outer, inner):
    rest = x.shape[1:]
    x = x.reshape((outer, inner, TILE) + rest)
    return jnp.swapaxes(x, 0, 1).reshape((outer * inner * TILE,) + rest)


def local(kernel):
    grid_rows = lax.axis_size("row")
    grid_cols = lax.axis_size("col")
    my_row = lax.axis_index("row")
    my_col = lax.axis_index("col")
    rows_loc, cols_loc = kernel.shape
    lead = PANELS * PANEL
    lead_rt = lead // (TILE * grid_rows)
    lead_ct = lead // (TILE * grid_cols)
    lead_r = lead_rt * TILE
    lead_c = lead_ct * TILE

    row_local = jnp.arange(rows_loc, dtype=jnp.int32)
    row_ids = (row_local // TILE * grid_rows + my_row) * TILE + row_local % TILE
    col_local = jnp.arange(cols_loc, dtype=jnp.int32)
    col_ids = (col_local // TILE * grid_cols + my_col) * TILE + col_local % TILE

    piece = kernel[:lead_r, :lead_c].reshape(lead_r, lead_ct, TILE).transpose(1, 0, 2)
    piece = lax.all_gather(piece, "col", axis=2, tiled=True)
    corner = piece.transpose(1, 0, 2).reshape(lead_r, lead)
    corner = lax.all_gather(corner, "row", axis=0, tiled=True)
    corner, rows_src, cols_src = lax.optimization_barrier(
        (corner, kernel[:lead_r, :], kernel[:, :lead_c])
    )
    a_lead = tiles_to_matrix(corner, grid_rows, lead_rt)

    cols_part = lax.all_gather(cols_src, "col", axis=1, tiled=True)
    x_rows_t = tiles_to_matrix(cols_part.T, grid_cols, lead_ct)

    linv = chol_inv(a_lead)
    x_rows_t, rows_src, linv = lax.optimization_barrier((x_rows_t, rows_src, linv))
    rows_part = lax.all_gather(rows_src, "row", axis=0, tiled=True)
    y_cols = tiles_to_matrix(rows_part, grid_rows, lead_rt)

    l0inv = linv[:PANEL, :PANEL]
    l1row = linv[PANEL:, :]

    def factor(panel_t, ids):
        g0 = mm(l0inv, panel_t[:PANEL])
        g1 = mm(l1row, panel_t)
        g1 = jnp.where(ids[None, :] >= PANEL, g1, 0.0)
        return jnp.concatenate([g0, g1], axis=0)

    g_rows = factor(x_rows_t, row_ids)
    g_cols = factor(y_cols, col_ids)

    schur = kernel - mm_tn(g_rows, g_cols, lax.Precision.HIGH)
    keep = (row_ids[:, None] >= lead) & (col_ids[None, :] >= lead)
    trailing = jnp.where(keep, schur, 0.0)
    per_col = lead // grid_cols
    factor_out = lax.dynamic_slice_in_dim(g_rows, my_col * per_col, per_col, 0)
    return (trailing, factor_out)


def solution(mesh):
    return jax.shard_map(
        local,
        mesh=mesh,
        in_specs=(P("row", "col"),),
        out_specs=(P("row", "col"), P("col", "row")),
        check_vma=False,
    )
```

```python
import jax
import jax.numpy as jnp
from jax import lax
from jax.experimental import pallas as pl
from jax.experimental.pallas import tpu as pltpu
from jax.sharding import PartitionSpec as P

PANEL = 512
PANELS = 2
TILE = 32
BLK = 128
KCOL = 8

HIGHEST = lax.Precision.HIGHEST


def _mm(a, b):
    return jnp.dot(a, b, precision=HIGHEST, preferred_element_type=jnp.float32)


def _diag_factor(d, lt_ref, w_ref):
    sub_all = lax.broadcasted_iota(jnp.int32, (BLK, BLK), 0)
    lane_all = lax.broadcasted_iota(jnp.int32, (BLK, BLK), 1)
    lane_row = lax.broadcasted_iota(jnp.int32, (1, BLK), 1)
    dm = d
    wm = (sub_all == lane_all).astype(jnp.float32)
    part = 16
    for q in range(BLK // part):
        lo = q * part
        rows = BLK - lo
        sub = lax.broadcasted_iota(jnp.int32, (rows, BLK), 0) + lo
        lane = lax.broadcasted_iota(jnp.int32, (rows, BLK), 1)

        def step(t, carry, sub=sub, lane=lane, lo=lo):
            dq, wq = carry
            j = lo + KCOL * t
            sels = [sub == j + m for m in range(KCOL)]
            rr = [jnp.sum(jnp.where(s, dq, 0.0), axis=0, keepdims=True) for s in sels]
            cc = [jnp.sum(jnp.where(lane == j + m, dq, 0.0), axis=1, keepdims=True) for m in range(KCOL)]
            wr = [jnp.sum(jnp.where(s, wq, 0.0), axis=0, keepdims=True) for s in sels]
            lk = [[None] * KCOL for _ in range(KCOL)]
            inv = [None] * KCOL
            for m in range(KCOL):
                for p in range(m + 1):
                    v = jnp.sum(jnp.where(lane_row == j + p, rr[m], 0.0), axis=1, keepdims=True)
                    for q in range(p):
                        v = v - lk[m][q] * lk[p][q]
                    if p < m:
                        lk[m][p] = v * inv[p]
                    else:
                        inv[m] = lax.rsqrt(v)
            lrow, lcol, wj = [], [], []
            for m in range(KCOL):
                rv, cv, wv = rr[m], cc[m], wr[m]
                for p in range(m):
                    rv = rv - lk[m][p] * lrow[p]
                    cv = cv - lk[m][p] * lcol[p]
                    wv = wv - lk[m][p] * wj[p]
                lrow.append(jnp.where(lane_row >= j + m, rv * inv[m], 0.0))
                lcol.append(jnp.where(sub[:, 0:1] > j + m, cv * inv[m], 0.0))
                wj.append(wv * inv[m])
            for m in range(KCOL):
                dq = dq - lcol[m] * lrow[m]
                wq = wq - lcol[m] * wj[m]
            for m in range(KCOL):
                wq = jnp.where(sels[m], wj[m], wq)
                lt_ref[pl.ds(j + m, 1), :] = lrow[m]
            return dq, wq

        dq, wq = lax.fori_loop(0, part // KCOL, step, (dm[lo:], wm[lo:]))
        w_ref[lo:lo + part, :] = wq[:part]
        if q + 1 < BLK // part:
            dm = jnp.concatenate([jnp.zeros((lo + part, BLK), jnp.float32), dq[part:]], axis=0)
            wm = jnp.concatenate([jnp.zeros((lo + part, BLK), jnp.float32), wq[part:]], axis=0)


def _chol_inv_kernel(a_ref, linv_ref, work, lt, dblk):
    n = a_ref.shape[0]
    nb = n // BLK
    work[...] = a_ref[...]
    linv_ref[...] = jnp.zeros_like(linv_ref)
    for k in range(nb):
        s = k * BLK
        _diag_factor(work[s:s + BLK, s:s + BLK], dblk, linv_ref.at[s:s + BLK, s:s + BLK])
        lt[s:s + BLK, s:s + BLK] = dblk[...]
        if k < nb - 1:
            e = s + BLK
            u = _mm(linv_ref[s:s + BLK, s:s + BLK], work[s:s + BLK, e:])
            lt[s:s + BLK, e:] = u
            work[e:, e:] = work[e:, e:] - _mm(u.T, u)
    for i in range(1, nb):
        s = i * BLK
        li = lt[0:s, s:s + BLK].T
        acc = _mm(li, linv_ref[0:s, 0:s])
        linv_ref[s:s + BLK, 0:s] = -_mm(linv_ref[s:s + BLK, s:s + BLK], acc)


def chol_inv(a):
    n = a.shape[0]
    return pl.pallas_call(
        _chol_inv_kernel,
        out_shape=jax.ShapeDtypeStruct((n, n), jnp.float32),
        in_specs=[pl.BlockSpec(memory_space=pltpu.VMEM)],
        out_specs=pl.BlockSpec(memory_space=pltpu.VMEM),
        scratch_shapes=[
            pltpu.VMEM((n, n), jnp.float32),
            pltpu.VMEM((n, n), jnp.float32),
            pltpu.VMEM((BLK, BLK), jnp.float32),
        ],
        compiler_params=pltpu.CompilerParams(vmem_limit_bytes=60 * 1024 * 1024),
    )(a)


def mm(a, b):
    return jnp.dot(a, b, precision=HIGHEST, preferred_element_type=jnp.float32)


def mm_tn(a, b, precision=HIGHEST):
    return lax.dot_general(
        a, b, (((0,), (0,)), ((), ())), precision=precision, preferred_element_type=jnp.float32
    )


def tiles_to_matrix(x, outer, inner):
    rest = x.shape[1:]
    x = x.reshape((outer, inner, TILE) + rest)
    return jnp.swapaxes(x, 0, 1).reshape((outer * inner * TILE,) + rest)


def local(kernel):
    grid_rows = lax.axis_size("row")
    grid_cols = lax.axis_size("col")
    my_row = lax.axis_index("row")
    my_col = lax.axis_index("col")
    rows_loc, cols_loc = kernel.shape
    lead = PANELS * PANEL
    lead_rt = lead // (TILE * grid_rows)
    lead_ct = lead // (TILE * grid_cols)
    lead_r = lead_rt * TILE
    lead_c = lead_ct * TILE

    row_local = jnp.arange(rows_loc, dtype=jnp.int32)
    row_ids = (row_local // TILE * grid_rows + my_row) * TILE + row_local % TILE
    col_local = jnp.arange(cols_loc, dtype=jnp.int32)
    col_ids = (col_local // TILE * grid_cols + my_col) * TILE + col_local % TILE

    piece = kernel[:lead_r, :lead_c].reshape(lead_r, lead_ct, TILE).transpose(1, 0, 2)
    piece = lax.all_gather(piece, "col", axis=2, tiled=True)
    corner = piece.transpose(1, 0, 2).reshape(lead_r, lead)
    corner = lax.all_gather(corner, "row", axis=0, tiled=True)
    corner, rows_src, cols_src = lax.optimization_barrier(
        (corner, kernel[:lead_r, :], kernel[:, :lead_c])
    )
    a_lead = tiles_to_matrix(corner, grid_rows, lead_rt)

    cols_part = lax.all_gather(cols_src, "col", axis=1, tiled=True)
    x_rows_t = tiles_to_matrix(cols_part.T, grid_cols, lead_ct)

    linv = chol_inv(a_lead)
    x_rows_t, rows_src, linv = lax.optimization_barrier((x_rows_t, rows_src, linv))
    rows_part = lax.all_gather(rows_src, "row", axis=0, tiled=True)
    y_cols = tiles_to_matrix(rows_part, grid_rows, lead_rt)

    l0inv = linv[:PANEL, :PANEL]
    l1row = linv[PANEL:, :]

    def factor(panel_t, ids):
        g0 = mm(l0inv, panel_t[:PANEL])
        g1 = mm(l1row, panel_t)
        g1 = jnp.where(ids[None, :] >= PANEL, g1, 0.0)
        return jnp.concatenate([g0, g1], axis=0)

    g_rows = factor(x_rows_t, row_ids)
    g_cols = factor(y_cols, col_ids)

    schur = kernel - mm_tn(g_rows, g_cols, lax.Precision.HIGH)
    keep = (row_ids[:, None] >= lead) & (col_ids[None, :] >= lead)
    trailing = jnp.where(keep, schur, 0.0)
    per_col = lead // grid_cols
    factor_out = lax.dynamic_slice_in_dim(g_rows, my_col * per_col, per_col, 0)
    return (trailing, factor_out)


def solution(mesh):
    return jax.shard_map(
        local,
        mesh=mesh,
        in_specs=(P("row", "col"),),
        out_specs=(P("row", "col"), P("col", "row")),
        check_vma=False,
    )
```

```python
import jax
import jax.numpy as jnp
from jax import lax
from jax.experimental import pallas as pl
from jax.experimental.pallas import tpu as pltpu
from jax.sharding import PartitionSpec as P

PANEL = 512
PANELS = 2
TILE = 32
BLK = 128
KCOL = 8

HIGHEST = lax.Precision.HIGHEST


def _mm(a, b):
    return jnp.dot(a, b, precision=HIGHEST, preferred_element_type=jnp.float32)


def _diag_factor(d, lt_ref, w_ref):
    sub_all = lax.broadcasted_iota(jnp.int32, (BLK, BLK), 0)
    lane_all = lax.broadcasted_iota(jnp.int32, (BLK, BLK), 1)
    lane_row = lax.broadcasted_iota(jnp.int32, (1, BLK), 1)
    dm = d
    wm = (sub_all == lane_all).astype(jnp.float32)
    part = 8
    for q in range(BLK // part):
        lo = q * part
        rows = BLK - lo
        sub = lax.broadcasted_iota(jnp.int32, (rows, BLK), 0) + lo
        lane = lax.broadcasted_iota(jnp.int32, (rows, BLK), 1)

        def step(t, carry, sub=sub, lane=lane, lo=lo):
            dq, wq = carry
            j = lo + KCOL * t
            sels = [sub == j + m for m in range(KCOL)]
            rr = [jnp.sum(jnp.where(s, dq, 0.0), axis=0, keepdims=True) for s in sels]
            cc = [jnp.sum(jnp.where(lane == j + m, dq, 0.0), axis=1, keepdims=True) for m in range(KCOL)]
            wr = [jnp.sum(jnp.where(s, wq, 0.0), axis=0, keepdims=True) for s in sels]
            lk = [[None] * KCOL for _ in range(KCOL)]
            inv = [None] * KCOL
            for m in range(KCOL):
                for p in range(m + 1):
                    v = jnp.sum(jnp.where(lane_row == j + p, rr[m], 0.0), axis=1, keepdims=True)
                    for q in range(p):
                        v = v - lk[m][q] * lk[p][q]
                    if p < m:
                        lk[m][p] = v * inv[p]
                    else:
                        inv[m] = lax.rsqrt(v)
            lrow, lcol, wj = [], [], []
            for m in range(KCOL):
                rv, cv, wv = rr[m], cc[m], wr[m]
                for p in range(m):
                    rv = rv - lk[m][p] * lrow[p]
                    cv = cv - lk[m][p] * lcol[p]
                    wv = wv - lk[m][p] * wj[p]
                lrow.append(jnp.where(lane_row >= j + m, rv * inv[m], 0.0))
                lcol.append(jnp.where(sub[:, 0:1] > j + m, cv * inv[m], 0.0))
                wj.append(wv * inv[m])
            for m in range(KCOL):
                dq = dq - lcol[m] * lrow[m]
                wq = wq - lcol[m] * wj[m]
            for m in range(KCOL):
                wq = jnp.where(sels[m], wj[m], wq)
                lt_ref[pl.ds(j + m, 1), :] = lrow[m]
            return dq, wq

        dq, wq = lax.fori_loop(0, part // KCOL, step, (dm[lo:], wm[lo:]))
        w_ref[lo:lo + part, :] = wq[:part]
        if q + 1 < BLK // part:
            dm = jnp.concatenate([jnp.zeros((lo + part, BLK), jnp.float32), dq[part:]], axis=0)
            wm = jnp.concatenate([jnp.zeros((lo + part, BLK), jnp.float32), wq[part:]], axis=0)


def _chol_inv_kernel(a_ref, linv_ref, work, lt, dblk):
    n = a_ref.shape[0]
    nb = n // BLK
    work[...] = a_ref[...]
    linv_ref[...] = jnp.zeros_like(linv_ref)
    for k in range(nb):
        s = k * BLK
        _diag_factor(work[s:s + BLK, s:s + BLK], dblk, linv_ref.at[s:s + BLK, s:s + BLK])
        lt[s:s + BLK, s:s + BLK] = dblk[...]
        if k < nb - 1:
            e = s + BLK
            u = _mm(linv_ref[s:s + BLK, s:s + BLK], work[s:s + BLK, e:])
            lt[s:s + BLK, e:] = u
            work[e:, e:] = work[e:, e:] - _mm(u.T, u)
    for i in range(1, nb):
        s = i * BLK
        li = lt[0:s, s:s + BLK].T
        acc = _mm(li, linv_ref[0:s, 0:s])
        linv_ref[s:s + BLK, 0:s] = -_mm(linv_ref[s:s + BLK, s:s + BLK], acc)


def chol_inv(a):
    n = a.shape[0]
    return pl.pallas_call(
        _chol_inv_kernel,
        out_shape=jax.ShapeDtypeStruct((n, n), jnp.float32),
        in_specs=[pl.BlockSpec(memory_space=pltpu.VMEM)],
        out_specs=pl.BlockSpec(memory_space=pltpu.VMEM),
        scratch_shapes=[
            pltpu.VMEM((n, n), jnp.float32),
            pltpu.VMEM((n, n), jnp.float32),
            pltpu.VMEM((BLK, BLK), jnp.float32),
        ],
        compiler_params=pltpu.CompilerParams(vmem_limit_bytes=60 * 1024 * 1024),
    )(a)


def mm(a, b):
    return jnp.dot(a, b, precision=HIGHEST, preferred_element_type=jnp.float32)


def mm_tn(a, b, precision=HIGHEST):
    return lax.dot_general(
        a, b, (((0,), (0,)), ((), ())), precision=precision, preferred_element_type=jnp.float32
    )


def tiles_to_matrix(x, outer, inner):
    rest = x.shape[1:]
    x = x.reshape((outer, inner, TILE) + rest)
    return jnp.swapaxes(x, 0, 1).reshape((outer * inner * TILE,) + rest)


def local(kernel):
    grid_rows = lax.axis_size("row")
    grid_cols = lax.axis_size("col")
    my_row = lax.axis_index("row")
    my_col = lax.axis_index("col")
    rows_loc, cols_loc = kernel.shape
    lead = PANELS * PANEL
    lead_rt = lead // (TILE * grid_rows)
    lead_ct = lead // (TILE * grid_cols)
    lead_r = lead_rt * TILE
    lead_c = lead_ct * TILE

    row_local = jnp.arange(rows_loc, dtype=jnp.int32)
    row_ids = (row_local // TILE * grid_rows + my_row) * TILE + row_local % TILE
    col_local = jnp.arange(cols_loc, dtype=jnp.int32)
    col_ids = (col_local // TILE * grid_cols + my_col) * TILE + col_local % TILE

    piece = kernel[:lead_r, :lead_c].reshape(lead_r, lead_ct, TILE).transpose(1, 0, 2)
    piece = lax.all_gather(piece, "col", axis=2, tiled=True)
    corner = piece.transpose(1, 0, 2).reshape(lead_r, lead)
    corner = lax.all_gather(corner, "row", axis=0, tiled=True)
    corner, rows_src, cols_src = lax.optimization_barrier(
        (corner, kernel[:lead_r, :], kernel[:, :lead_c])
    )
    a_lead = tiles_to_matrix(corner, grid_rows, lead_rt)

    cols_part = lax.all_gather(cols_src, "col", axis=1, tiled=True)
    x_rows_t = tiles_to_matrix(cols_part.T, grid_cols, lead_ct)

    linv = chol_inv(a_lead)
    x_rows_t, rows_src, linv = lax.optimization_barrier((x_rows_t, rows_src, linv))
    rows_part = lax.all_gather(rows_src, "row", axis=0, tiled=True)
    y_cols = tiles_to_matrix(rows_part, grid_rows, lead_rt)

    l0inv = linv[:PANEL, :PANEL]
    l1row = linv[PANEL:, :]

    def factor(panel_t, ids, precision=HIGHEST):
        g0 = jnp.dot(l0inv, panel_t[:PANEL], precision=precision, preferred_element_type=jnp.float32)
        g1 = jnp.dot(l1row, panel_t, precision=precision, preferred_element_type=jnp.float32)
        g1 = jnp.where(ids[None, :] >= PANEL, g1, 0.0)
        return jnp.concatenate([g0, g1], axis=0)

    g_rows = factor(x_rows_t, row_ids)
    g_cols = factor(y_cols, col_ids, lax.Precision.HIGH)

    schur = kernel - mm_tn(g_rows, g_cols, lax.Precision.HIGH)
    keep = (row_ids[:, None] >= lead) & (col_ids[None, :] >= lead)
    trailing = jnp.where(keep, schur, 0.0)
    per_col = lead // grid_cols
    factor_out = lax.dynamic_slice_in_dim(g_rows, my_col * per_col, per_col, 0)
    return (trailing, factor_out)


def solution(mesh):
    return jax.shard_map(
        local,
        mesh=mesh,
        in_specs=(P("row", "col"),),
        out_specs=(P("row", "col"), P("col", "row")),
        check_vma=False,
    )
```
